256 devices in a mesh: stream: 16 (over z_hi, y, core), lat: 16 (over z_lo, x).
Axes of the slice: x: 4, y: 4, z: 8 (z_hi: 2, z_lo: 4; z = z_hi * 4 + z_lo), core: 2. Of those that a mesh axis runs over, the one named last changes fastest.
Arguments:
- inverse: bfloat16 [32, 16, 4, 512, 512], P('lat', 'stream'), may hold values from -2 to 2
- upwind: bfloat16 [32, 16, 4, 64, 512], P('lat', 'stream'), may hold values from -0.75 to 0.75
- lateral: bfloat16 [32, 16, 4, 64, 512], P('lat', 'stream'), may hold values from -0.375 to 0.375
- inlet_trace: float32 [32, 64, 256], P('lat'), may hold values from -6 to 6
- previous: bfloat16 [32, 16, 4, 512, 256], P('lat', 'stream'), may hold values from -6 to 6
- uptake_rate: float32 [256], replicated, may hold values from 0.3 to 3
- affinity: float32 [256], replicated, may hold values from 0.5 to 4
- flow_order: int32 [32, 16, 4], P('lat', 'stream'), may hold values from 0 to 3, each once within a row
Outputs:
- concentration: bfloat16 [32, 16, 4, 512, 256], P('lat', 'stream')
The draws below stay inside these ranges and needn't reach their ends.
Inputs may be any that keep to these rules, and one draw needn't show every extreme that they name: `flow_order`: each row of 4 entries lists 0 to 3 once each.
All inputs are finite; a program needn't handle non-finite values.
Results may differ from the reference program's by a relative error of at most 0.002.
Values sent between devices are 32-bit elements; how exact they have to be, the bound alone decides.
A program may use at most 64 MiB of HBM per device.

```python
import math
import jax
import jax.numpy as jnp
from jax import lax

NODES_1D = 8
NODES = 512
FACE = 64
TRACERS = 256
ROW_DEV = 4
ITERS = 2
COLS = 32
BLOCKS = 16


def draw_inverse(key, part):
    first_key, second_key = jax.random.split(jax.random.fold_in(key, 11))
    full_shape = (COLS, BLOCKS, ROW_DEV, NODES, NODES)
    diagonal = jnp.exp(jax.random.uniform(first_key, full_shape[:-1], jnp.float32, math.log(0.8), math.log(1.25)))
    spread_part = 0.4 * jax.random.normal(second_key, full_shape, jnp.float32) / math.sqrt(NODES)
    unit_matrix = jnp.eye(NODES, dtype=jnp.float32)
    return (spread_part + diagonal[..., None] * unit_matrix).astype(jnp.bfloat16)


def level_of(own_key, dims, shards, least, largest):
    factor_of, own = 1.0, jax.random.fold_in(own_key, 6)
    for dim, parts in shards:
        steps = jnp.exp(jax.random.uniform(jax.random.fold_in(own, dim), (parts,), jnp.float32, least / len(shards), largest / len(shards)))
        factor_of = factor_of * jnp.repeat(steps, dims[dim] // parts).reshape([-1 if axis == dim else 1 for axis in range(len(dims))])
    return factor_of


def gaussian(key, shape, scale, limit, pieces=(), kind=jnp.bfloat16):
    entries = scale * jax.random.normal(key, shape, jnp.float32)
    if pieces:
        entries = entries * level_of(key, shape, pieces, -0.22, 0.18)
    return jnp.clip(entries, -limit, limit).astype(kind)


def setup_inputs(seed: int = 0) -> dict:
    key_of = jax.random.split(jax.random.key(seed), 9)
    inverse = draw_inverse(jax.random.fold_in(key_of[8], 71), 0)
    upwind = gaussian(key_of[1], (COLS, BLOCKS, ROW_DEV, FACE, NODES), (0.9 / NODES_1D), 0.75, ((0, 16), (1, 16)))
    lateral = gaussian(key_of[2], (COLS, BLOCKS, ROW_DEV, FACE, NODES), (0.5 / NODES_1D), 0.375, ((0, 16), (1, 16)))
    inlet_trace = gaussian(key_of[3], (COLS, FACE, TRACERS), 1.0, 6.0, ((0, 16),), jnp.float32)
    previous = gaussian(key_of[4], (COLS, BLOCKS, ROW_DEV, NODES, TRACERS), 1.0, 6.0, ((0, 16), (1, 16)))
    uptake_rate = jnp.clip(jnp.exp(jax.random.uniform(key_of[5], (TRACERS,), jnp.float32, math.log(0.3), math.log(3.0))), 0.3, 3.0)
    affinity = jnp.clip(jnp.exp(jax.random.uniform(key_of[6], (TRACERS,), jnp.float32, math.log(0.5), math.log(4.0))), 0.5, 4.0)
    flow_order = jax.vmap(lambda own: jax.random.permutation(own, ROW_DEV))(jax.random.split(key_of[7], COLS * BLOCKS)).reshape((COLS, BLOCKS, ROW_DEV)).astype(jnp.int32)
    return {"inverse": inverse, "upwind": upwind, "lateral": lateral, "inlet_trace": inlet_trace, "previous": previous, "uptake_rate": uptake_rate, "affinity": affinity, "flow_order": flow_order}


HIGHEST = lax.Precision.HIGHEST


def lateral_face(nodal_field):
    leading = nodal_field.shape[:-2]
    shaped = nodal_field.reshape(leading + (NODES_1D, NODES_1D, NODES_1D, TRACERS))
    return shaped[..., :, NODES_1D - 1, :, :].reshape(leading + (FACE, TRACERS))


def langmuir(lagged, uptake_rate, affinity):
    return uptake_rate * lagged / (1.0 + affinity * jnp.abs(lagged))


def reference(inverse, upwind, lateral, inlet_trace, previous, uptake_rate, affinity, flow_order):
    current = previous.astype(jnp.float32)
    columns = jnp.arange(COLS)
    for sweep_index in range(ITERS):
        lagged = current
        traces = lateral_face(lagged)
        lateral_in = jnp.concatenate([jnp.zeros_like(traces[:1]), traces[:-1]], axis=0)

        def block_step(inflow, block_index):
            order_block = lax.dynamic_index_in_dim(flow_order, block_index, 1, False)
            inverse_block = lax.dynamic_index_in_dim(inverse, block_index, 1, False)
            upwind_block = lax.dynamic_index_in_dim(upwind, block_index, 1, False)
            lateral_block = lax.dynamic_index_in_dim(lateral, block_index, 1, False)
            lagged_block = lax.dynamic_index_in_dim(lagged, block_index, 1, False)
            side_block = lax.dynamic_index_in_dim(lateral_in, block_index, 1, False)

            def element_step(carried, position):
                chosen = lax.dynamic_index_in_dim(order_block, position, 1, False).astype(jnp.int32)
                matrix = inverse_block[columns, chosen].astype(jnp.float32)
                up_part = upwind_block[columns, chosen].astype(jnp.float32)
                side_part = lateral_block[columns, chosen].astype(jnp.float32)
                source = langmuir(lagged_block[columns, chosen], uptake_rate, affinity)
                right_side = source + jnp.einsum('cfn,cfg->cng', side_part, side_block[columns, chosen], precision=HIGHEST)
                right_side = right_side + jnp.einsum('cfn,cfg->cng', up_part, carried, precision=HIGHEST)
                solved = jnp.einsum('cmn,cng->cmg', matrix, right_side, precision=HIGHEST)
                return solved[:, NODES - FACE:, :], solved

            outflow, solved_all = lax.scan(element_step, inflow, jnp.arange(ROW_DEV))
            placed = jnp.moveaxis(solved_all, 0, 1)
            storage_rank = jnp.argsort(order_block, axis=1).astype(jnp.int32)
            stored = jnp.take_along_axis(placed, storage_rank[:, :, None, None], axis=1)
            return outflow, stored

        final_trace, blocks_out = lax.scan(block_step, inlet_trace, jnp.arange(BLOCKS))
        current = jnp.moveaxis(blocks_out, 0, 1)
    return current.astype(jnp.bfloat16)
```

```python
import functools

import jax
import jax.numpy as jnp
from jax import lax
from jax.experimental import pallas as pl
from jax.experimental.pallas import tpu as pltpu
from jax.sharding import PartitionSpec as P

MESH = pl.DeviceIdType.MESH
F32 = jnp.float32
BF16 = jnp.bfloat16
YS = 4


def split(x):
    hi = x.astype(BF16)
    return hi, (x - hi.astype(F32)).astype(BF16)


def dot(a, b):
    return jnp.dot(a, b, preferred_element_type=F32)


def dot_nt(a, b):
    return lax.dot_general(a, b, (((1,), (1,)), ((), ())), preferred_element_type=F32)


def dot3(ah, al, b):
    bh, bl = split(b)
    return dot(ah, bh) + (dot(al, bh) + dot(ah, bl))


def cat0(*xs):
    return jnp.concatenate(xs, axis=0)


def kernel(
    order, inv, up, side, inlet, prev, upt, aff, out,
    A, UL, PV, MN, F, SRC, LS, LR, LAT, H, G, INF, TT, TP, TC, THL, VV,
    OS, OR, OC, X8S, X8R, YSND, XIN,
    ld_sem, lat_s, lat_r, t_s, t_r, tc_s, tc_r, s1_s, s1_r, s2_s, s2_r, z_s, z_r, s4_s, s4_r,
):
    cols, rows, nodes, face = 2, 4, 512, 64
    half = 128
    edge = nodes - face
    s = lax.axis_index("stream")
    lat = lax.axis_index("lat")
    lats = lax.axis_size("lat")
    core = lax.rem(s, 2)
    y = lax.rem(s // 2, YS)
    zhi = s // (2 * YS)
    is0 = core == 0
    partner = {"stream": s + 1 - 2 * core}

    def ypeer(d):
        return {"stream": zhi * (2 * YS) + lax.rem(y + d, YS) * 2 + core}

    zpeer = {"stream": lax.rem(s + 2 * YS, 4 * YS)}

    loads = {}

    def load(name, k, src, dst):
        c = pltpu.make_async_copy(src, dst, ld_sem.at[k])
        c.start()
        loads[name] = c

    load("prev1", 0, prev.at[1, 0], PV.at[1])
    load("u0", 2, up.at[0, 0], UL.at[0, :, 0:face])
    load("l0", 4, side.at[0, 0], UL.at[0, :, face:])
    load("al0", 6, inv.at[0, 0, :, edge:], A.at[0, :, edge:])
    load("u1", 3, up.at[1, 0], UL.at[1, :, 0:face])
    load("l1", 5, side.at[1, 0], UL.at[1, :, face:])
    load("al1", 7, inv.at[1, 0, :, edge:], A.at[1, :, edge:])
    load("prev0", 1, prev.at[0, 0], PV.at[0])
    load("ar1", 9, inv.at[1, 0, :, 0:edge], A.at[1, :, 0:edge])
    load("ar0", 8, inv.at[0, 0, :, 0:edge], A.at[0, :, 0:edge])

    barrier = pltpu.get_barrier_semaphore()
    peers = [partner, ypeer(1), ypeer(2), ypeer(3), zpeer]
    peers += [{"lat": lax.rem(lat + 1, lats)}, {"lat": lax.rem(lat + lats - 1, lats)}]
    for peer in peers:
        pl.semaphore_signal(barrier, inc=1, device_id=peer, device_id_type=MESH)

    def remote(src, dst, ssem, rsem, peer):
        return pltpu.make_async_remote_copy(
            src_ref=src, dst_ref=dst, send_sem=ssem, recv_sem=rsem, device_id=peer, device_id_type=MESH
        )

    def lat_copy(it):
        return remote(LS.at[it], LR.at[it], lat_s.at[it], lat_r.at[it], {"lat": lax.rem(lat + 1, lats)})

    def lat_send(it):
        @pl.when(lat < lats - 1)
        def _():
            lat_copy(it).start()

    def prev_trace(c, j):
        parts = []
        for a in range(8):
            piece = PV[c, j, a * 64 + 48 : a * 64 + 64, :].astype(F32)
            parts.append(piece[8:16])
        return cat0(*parts)

    def value_trace(x):
        return cat0(*[x[a * 64 + 56 : a * 64 + 64] for a in range(8)])

    loads["prev1"].wait()
    for j in range(rows):
        LS[0, j] = prev_trace(1, j)
    pl.semaphore_wait(barrier, len(peers))
    lat_send(0)

    for c in range(cols):
        for n in ("u", "l", "al"):
            loads[n + str(c)].wait()
        for j in range(rows):
            hi, lo = split(dot_nt(A[c, j, edge:, :], UL[c, j]))
            MN[c, j, edge:, 0:128] = hi
            MN[c, j, edge:, 128:256] = lo

    def mn_edge(c, j):
        return MN[c, j, edge:, :]

    def apply(mn4, rh, rl):
        return dot(mn4, cat0(rh, rh)) + dot(mn4[:, 0:128], rl)

    zero64 = jnp.zeros((face, face), BF16)
    for c in range(cols):
        first = mn_edge(c, order[c, 0, 0])
        g = first[:, 0:face].astype(F32) + first[:, 128 : 128 + face].astype(F32)
        for p in range(1, rows + 1):
            gh, gl = split(g)
            if p < rows:
                G[c, 0, (p - 1) * face : p * face, :] = gh
                G[c, 1, (p - 1) * face : p * face, :] = gl
                g = apply(mn_edge(c, order[c, 0, p]), cat0(gh, zero64), cat0(gl, zero64))
        TT[c] = g
    t_copy = remote(TT, TP, t_s, t_r, partner)
    t_copy.start()

    loads["prev0"].wait()
    for j in range(rows):
        LAT[0, 1, j] = prev_trace(0, j).astype(BF16)
        LAT[1, 1, j] = jnp.zeros((face, 256), BF16)
    for c in range(cols):
        piece = jnp.where(is0, inlet[c, :, 0:half], inlet[c, :, half:])
        piece = jnp.where(zhi == 0, piece, jnp.zeros_like(piece))
        for it in range(2):
            OC[it, c, YS] = piece

    rate = upt[...].reshape(1, 256)
    affinity = aff[...].reshape(1, 256)

    def source_of(x):
        return rate * x / (1.0 + affinity * jnp.abs(x))

    def put_source(c, j, x):
        hi, lo = split(source_of(x))
        SRC[c, 0, j] = hi
        SRC[c, 1, j] = lo
        a = A[c, j, edge:, :]
        F[c, j, edge:, :] = dot(a, hi) + dot(a, lo)

    def first_source(c):
        def body(j, _):
            put_source(c, j, PV[c, j].astype(F32))
            return 0

        lax.fori_loop(0, rows, body, 0)

    def rest(c):
        def body(j, _):
            a = A[c, j, 0:edge, :]
            F[c, j, 0:edge, :] = dot(a, SRC[c, 0, j]) + dot(a, SRC[c, 1, j])
            return 0

        lax.fori_loop(0, rows, body, 0)

    def maps_rest(c):
        def body(j, _):
            hi, lo = split(dot_nt(A[c, j, 0:edge, :], UL[c, j]))
            MN[c, j, 0:edge, 0:128] = hi
            MN[c, j, 0:edge, 128:256] = lo
            return 0

        lax.fori_loop(0, rows, body, 0)

    zero_trace = jnp.zeros((face, 256), BF16)

    def s1_copy(it, c):
        return remote(OS.at[it, c, 1 - core], OR.at[it, c], s1_s.at[it, c], s1_r.at[it, c], partner)

    def chain(it, c):
        drive = []
        for p in range(rows):
            j = order[c, 0, p]
            lh, ll = LAT[0, c, j], LAT[1, c, j]
            drive.append(F[c, j, edge:, :] + apply(mn_edge(c, j), cat0(zero_trace, lh), cat0(zero_trace, ll)))
        h = drive[0]
        for p in range(1, rows):
            H[c, p - 1] = h
            hh, hl = split(h)
            h = drive[p] + apply(mn_edge(c, order[c, 0, p]), cat0(hh, zero_trace), cat0(hl, zero_trace))
        OS[it, c, 0] = h[:, 0:half]
        OS[it, c, 1] = h[:, half:]
        s1_copy(it, c).start()

    def first_second(it, c):
        own, got = OS[it, c, core], OR[it, c]
        return jnp.where(is0, own, got), jnp.where(is0, got, own)

    def s2_copy(it, c, d):
        return remote(OC.at[it, c, y], OC.at[it, c, y], s2_s.at[it, c, d - 1], s2_r.at[it, c, y], ypeer(d))

    def s2_arrival(it, c, d):
        source = lax.rem(y + d, YS)
        return remote(OC.at[it, c, source], OC.at[it, c, source], s2_s.at[it, c, d - 1], s2_r.at[it, c, source], ypeer(d))

    def compose(it, c):
        s1_copy(it, c).wait_recv()
        o_first, o_second = first_second(it, c)
        OC[it, c, y] = dot3(THL[1, c, 0], THL[1, c, 1], o_first) + o_second
        for d in (2, 1, 3):
            s2_copy(it, c, d).start()

    def z_copy(it, c):
        return remote(X8S.at[it, c], X8R.at[it, c], z_s.at[it, c], z_r.at[it, c], zpeer)

    def s4_copy(it, c):
        return remote(YSND.at[it, c], XIN.at[it, c, core], s4_s.at[it, c], s4_r.at[it, c], partner)

    def s4_arrival(it, c):
        return remote(YSND.at[it, c], XIN.at[it, c, 1 - core], s4_s.at[it, c], s4_r.at[it, c], partner)

    def put_entering(it, c, q):
        YSND[it, c] = jnp.where(is0, q[face:], q[0:face])
        XIN[it, c, core] = jnp.where(is0, q[0:face], q[face:])

    def gather(it, c):
        for d in (1, 3, 2):
            s2_arrival(it, c, d).wait_recv()
        offsets = OC[it, c].reshape((YS + 1) * face, half)
        q = dot3(VV[c, 0], VV[c, 1], offsets)
        o_first, _ = first_second(it, c)
        q = cat0(q[0:face], q[face : 2 * face] + o_first, q[2 * face :])

        @pl.when(zhi == 0)
        def _():
            X8S[it, c] = q[2 * face :]
            z_copy(it, c).start()
            put_entering(it, c, q[0 : 2 * face])
            s4_copy(it, c).start()

        @pl.when(zhi == 1)
        def _():
            X8S[it, c] = q[0:face]
            YSND[it, c] = q[face : 2 * face]

    def carry(it, c):
        @pl.when(zhi == 1)
        def _():
            z_copy(it, c).wait_recv()
            q = cat0(X8S[it, c], YSND[it, c])
            v = slice(YS * face, (YS + 1) * face)
            q = q + dot3(VV[c, 0, 0 : 2 * face, v], VV[c, 1, 0 : 2 * face, v], X8R[it, c])
            put_entering(it, c, q)
            s4_copy(it, c).start()

    def inflows(it, c):
        s4_arrival(it, c).wait_recv()
        x = jnp.concatenate([XIN[it, c, 0], XIN[it, c, 1]], axis=1)
        xh, xl = split(x)
        INF[0, c, 0] = xh
        INF[1, c, 0] = xl
        later = dot(G[c, 0], xh) + (dot(G[c, 1], xh) + dot(G[c, 0], xl))
        for p in range(1, rows):
            xh, xl = split(later[(p - 1) * face : p * face] + H[c, p - 1])
            INF[0, c, p] = xh
            INF[1, c, p] = xl

    def rank_of(c, j):
        rank = jnp.int32(0)
        for p in range(1, rows):
            rank = jnp.where(order[c, 0, p] == j, p, rank)
        return rank

    def solved(c, j):
        rank = rank_of(c, j)
        rh = cat0(INF[0, c, rank], LAT[0, c, j])
        rl = cat0(INF[1, c, rank], LAT[1, c, j])
        return F[c, j] + apply(MN[c, j], rh, rl)

    def lag(c):
        def body(j, _):
            x = solved(c, j)
            trace = value_trace(x)
            if c == 1:
                LS[1, j] = trace
            else:
                hi, lo = split(trace)
                LAT[0, 1, j] = hi
                LAT[1, 1, j] = lo
            put_source(c, j, x)
            return 0

        lax.fori_loop(0, rows, body, 0)

    def finish(c):
        def body(j, _):
            out[c, 0, j] = solved(c, j).astype(BF16)
            return 0

        lax.fori_loop(0, rows, body, 0)

    def lat_arrival(it):
        @pl.when(lat > 0)
        def _():
            lat_copy(it).wait_recv()
            for j in range(rows):
                hi, lo = split(LR[it, j])
                LAT[0, 0, j] = hi
                LAT[1, 0, j] = lo

        @pl.when(lat == 0)
        def _():
            for j in range(rows):
                LAT[0, 0, j] = zero_trace
                LAT[1, 0, j] = zero_trace

    first_source(1)

    t_copy.wait_recv()
    for c in range(cols):
        own, got = TT[c], TP[c]
        t0h, t0l = split(jnp.where(is0, own, got))
        t1h, t1l = split(jnp.where(is0, got, own))
        THL[0, c, 0], THL[0, c, 1], THL[1, c, 0], THL[1, c, 1] = t0h, t0l, t1h, t1l
        TC[y, c] = dot3(t1h, t1l, jnp.where(is0, own, got))

    def tc_copy(d):
        return remote(TC.at[y], TC.at[y], tc_s.at[d - 1], tc_r.at[y], ypeer(d))

    def tc_arrival(d):
        source = lax.rem(y + d, YS)
        return remote(TC.at[source], TC.at[source], tc_s.at[d - 1], tc_r.at[source], ypeer(d))

    for d in (2, 1, 3):
        tc_copy(d).start()

    chain(0, 1)
    first_source(0)
    compose(0, 1)

    for d in (1, 3, 2):
        tc_arrival(d).wait_recv()
    width = (YS + 1) * face
    row_id = lax.broadcasted_iota(jnp.int32, (face, width), 0)
    lane_id = lax.broadcasted_iota(jnp.int32, (face, width), 1)

    def unit(block):
        return jnp.where(lane_id - face * block == row_id, 1.0, 0.0).astype(F32)

    for c in range(cols):
        x = unit(YS)
        mine = jnp.where(y == 0, x, jnp.zeros_like(x))
        for t in range(YS):
            if t == 0:
                x = cat_lanes(TC[0, c], width) + unit(0)
            else:
                th, tl = split(TC[t, c])
                x = dot3(th, tl, x) + unit(t)
            if t + 1 < YS:
                mine = jnp.where(y == t + 1, x, mine)
        both = dot3(THL[0, c, 0], THL[0, c, 1], mine)
        vh, vl = split(cat0(mine, both, x))
        VV[c, 0] = vh
        VV[c, 1] = vl

    lat_arrival(0)
    chain(0, 0)
    loads["ar1"].wait()
    maps_rest(1)
    compose(0, 0)
    rest(1)
    gather(0, 1)
    loads["ar0"].wait()
    maps_rest(0)
    rest(0)
    gather(0, 0)
    carry(0, 1)
    inflows(0, 1)
    lag(1)
    lat_send(1)
    carry(0, 0)
    inflows(0, 0)
    lag(0)

    chain(1, 1)
    rest(1)
    compose(1, 1)
    lat_arrival(1)
    chain(1, 0)
    rest(0)
    compose(1, 0)
    gather(1, 1)
    carry(1, 1)
    gather(1, 0)
    carry(1, 0)
    inflows(1, 1)
    finish(1)
    inflows(1, 0)
    finish(0)

    t_copy.wait_send()
    for d in range(1, YS):
        tc_copy(d).wait_send()
    for it in range(2):
        for c in range(cols):
            s1_copy(it, c).wait_send()
            s4_copy(it, c).wait_send()
            for d in range(1, YS):
                s2_copy(it, c, d).wait_send()

            @pl.when(zhi == 0)
            def _():
                z_copy(it, c).wait_send()

        @pl.when(lat < lats - 1)
        def _():
            lat_copy(it).wait_send()


def cat_lanes(t, width):
    face = t.shape[0]
    return jnp.concatenate([jnp.zeros((face, width - face), F32), t], axis=1)


def per_device(inverse, upwind, lateral, inlet_trace, previous, uptake_rate, affinity, flow_order):
    any_space = pl.BlockSpec(memory_space=pltpu.HBM)
    vmem = pl.BlockSpec(memory_space=pltpu.VMEM)
    dma = pltpu.SemaphoreType.DMA
    scratch = [
        pltpu.VMEM((2, 4, 512, 512), BF16),
        pltpu.VMEM((2, 4, 128, 512), BF16),
        pltpu.VMEM((2, 4, 512, 256), BF16),
        pltpu.VMEM((2, 4, 512, 256), BF16),
        pltpu.VMEM((2, 4, 512, 256), F32),
        pltpu.VMEM((2, 2, 4, 512, 256), BF16),
        pltpu.VMEM((2, 4, 64, 256), F32),
        pltpu.VMEM((2, 4, 64, 256), F32),
        pltpu.VMEM((2, 2, 4, 64, 256), BF16),
        pltpu.VMEM((2, 3, 64, 256), F32),
        pltpu.VMEM((2, 2, 192, 64), BF16),
        pltpu.VMEM((2, 2, 4, 64, 256), BF16),
        pltpu.VMEM((2, 64, 64), F32),
        pltpu.VMEM((2, 64, 64), F32),
        pltpu.VMEM((4, 2, 64, 64), F32),
        pltpu.VMEM((2, 2, 2, 64, 64), BF16),
        pltpu.VMEM((2, 2, 192, 320), BF16),
        pltpu.VMEM((2, 2, 2, 64, 128), F32),
        pltpu.VMEM((2, 2, 64, 128), F32),
        pltpu.VMEM((2, 2, 5, 64, 128), F32),
        pltpu.VMEM((2, 2, 64, 128), F32),
        pltpu.VMEM((2, 2, 64, 128), F32),
        pltpu.VMEM((2, 2, 64, 128), F32),
        pltpu.VMEM((2, 2, 2, 64, 128), F32),
        dma((10,)),
        dma((2,)), dma((2,)),
        dma, dma,
        dma((3,)), dma((4,)),
        dma((2, 2)), dma((2, 2)),
        dma((2, 2, 3)), dma((2, 2, 4)),
        dma((2, 2)), dma((2, 2)),
        dma((2, 2)), dma((2, 2)),
    ]
    return pl.pallas_call(
        kernel,
        out_shape=jax.ShapeDtypeStruct(previous.shape, BF16),
        in_specs=[
            pl.BlockSpec(memory_space=pltpu.SMEM),
            any_space, any_space, any_space, vmem, any_space, vmem, vmem,
        ],
        out_specs=vmem,
        scratch_shapes=scratch,
        compiler_params=pltpu.CompilerParams(
            collective_id=0, has_side_effects=True, vmem_limit_bytes=60 * 1024 * 1024
        ),
    )(flow_order, inverse, upwind, lateral, inlet_trace, previous, uptake_rate, affinity)


def solution(mesh):
    placed = (
        P("lat", "stream", None, None, None),
        P("lat", "stream", None, None, None),
        P("lat", "stream", None, None, None),
        P("lat", None, None),
        P("lat", "stream", None, None, None),
        P(),
        P(),
        P("lat", "stream", None),
    )
    return jax.shard_map(
        per_device,
        mesh=mesh,
        in_specs=placed,
        out_specs=P("lat", "stream", None, None, None),
        check_vma=False,
    )
```

```python
import functools

import jax
import jax.numpy as jnp
from jax import lax
from jax.experimental import pallas as pl
from jax.experimental.pallas import tpu as pltpu
from jax.sharding import PartitionSpec as P

MESH = pl.DeviceIdType.MESH
F32 = jnp.float32
BF16 = jnp.bfloat16
YS = 4


def split(x):
    hi = x.astype(BF16)
    return hi, (x - hi.astype(F32)).astype(BF16)


def dot(a, b):
    return jnp.dot(a, b, preferred_element_type=F32)


def dot_nt(a, b):
    return lax.dot_general(a, b, (((1,), (1,)), ((), ())), preferred_element_type=F32)


def dot3(ah, al, b):
    bh, bl = split(b)
    return dot(ah, bh) + (dot(al, bh) + dot(ah, bl))


def cat0(*xs):
    return jnp.concatenate(xs, axis=0)


def kernel(
    order_in, inv, up, side, inlet_in, prev, upt_in, aff_in, out,
    order, inlet, upt, aff, A, UL, PV, MM, NN, MT, F, SRC, LS, LR, LAT, H, G, INF, TT, TP, TC, THL, VV,
    OS, OR, OC, X8S, X8R, YSND, XIN,
    ld_sem, lat_s, lat_r, t_s, t_r, tc_s, tc_r, s1_s, s1_r, s2_s, s2_r, z_s, z_r, s4_s, s4_r,
):
    cols, rows, nodes, face = 2, 4, 512, 64
    half = 128
    edge = nodes - face
    s = lax.axis_index("stream")
    lat = lax.axis_index("lat")
    lats = lax.axis_size("lat")
    core = lax.rem(s, 2)
    y = lax.rem(s // 2, YS)
    zhi = s // (2 * YS)
    is0 = core == 0
    partner = {"stream": s + 1 - 2 * core}

    def ypeer(d):
        return {"stream": zhi * (2 * YS) + lax.rem(y + d, YS) * 2 + core}

    zpeer = {"stream": lax.rem(s + 2 * YS, 4 * YS)}

    loads = {}

    def load(name, k, src, dst):
        c = pltpu.make_async_copy(src, dst, ld_sem.at[k])
        c.start()
        loads[name] = c

    load("prev1", 0, prev.at[1, 0], PV.at[1])
    for c in (1, 0):
        for k in range(2):
            load(f"u{c}{k}", 2 + 2 * c + k, up.at[c, 0], UL.at[c, :, k * face : (k + 1) * face])
            load(f"l{c}{k}", 6 + 2 * c + k, side.at[c, 0], UL.at[c, :, (2 + k) * face : (3 + k) * face])
        load(f"al{c}", 10 + c, inv.at[c, 0, :, edge:], A.at[c, :, edge:])
        if c:
            load("order", 14, order_in, order)
            load("upt", 15, upt_in, upt)
            load("aff", 16, aff_in, aff)
            load("prev0", 1, prev.at[0, 0], PV.at[0])
    load("inlet", 17, inlet_in, inlet)
    load("ar1", 13, inv.at[1, 0, :, 0:edge], A.at[1, :, 0:edge])
    load("ar0", 12, inv.at[0, 0, :, 0:edge], A.at[0, :, 0:edge])

    barrier = pltpu.get_barrier_semaphore()

    def hello(peer):
        pl.semaphore_signal(barrier, inc=1, device_id=peer, device_id_type=MESH)

    for peer in (partner, ypeer(1), ypeer(2), ypeer(3)):
        hello(peer)

    @pl.when(lat > 0)
    def _():
        hello({"lat": lat - 1})

    @pl.when(zhi == 1)
    def _():
        hello(zpeer)

    expected = 4 + jnp.where(lat < lats - 1, 1, 0) + jnp.where(zhi == 0, 1, 0)

    def remote(src, dst, ssem, rsem, peer):
        return pltpu.make_async_remote_copy(
            src_ref=src, dst_ref=dst, send_sem=ssem, recv_sem=rsem, device_id=peer, device_id_type=MESH
        )

    def lat_copy(it):
        return remote(LS.at[it], LR.at[it], lat_s.at[it], lat_r.at[it], {"lat": lax.rem(lat + 1, lats)})

    def lat_send(it):
        @pl.when(lat < lats - 1)
        def _():
            lat_copy(it).start()

    def prev_trace(c, j):
        parts = []
        for a in range(8):
            piece = PV[c, j, a * 64 + 48 : a * 64 + 64, :].astype(F32)
            parts.append(piece[8:16])
        return cat0(*parts)

    def value_trace(x):
        return cat0(*[x[a * 64 + 56 : a * 64 + 64] for a in range(8)])

    def apply(m4, h, l):
        return dot(m4, cat0(h, l, h, l))

    def put_maps(c, j, rows_of):
        hi, lo = split(dot_nt(A[c, j, rows_of, :], UL[c, j]))
        MM[c, j, rows_of, 0:128] = hi[:, 0:128]
        MM[c, j, rows_of, 128:256] = lo[:, 0:128]
        NN[c, j, rows_of, 0:128] = hi[:, 128:256]
        NN[c, j, rows_of, 128:256] = lo[:, 128:256]

    def edge_maps(c):
        for n in (f"u{c}0", f"u{c}1", f"l{c}0", f"l{c}1", f"al{c}"):
            loads[n].wait()
        for j in range(rows):
            put_maps(c, j, slice(edge, nodes))

    loads["prev1"].wait()
    for j in range(rows):
        LS[0, j] = prev_trace(1, j)
    edge_maps(1)
    pl.semaphore_wait(barrier, expected)
    lat_send(0)

    edge_maps(0)
    loads["order"].wait()

    def mm_edge(c, j):
        return MM[c, j, edge:, :]

    for c in range(cols):
        first = mm_edge(c, order[c, 0, 0])
        g = first[:, 0:face].astype(F32) + first[:, 128 : 128 + face].astype(F32)
        for p in range(1, rows + 1):
            if p < rows:
                gh, gl = split(g)
                G[c, 0, (p - 1) * face : p * face, :] = gh
                G[c, 1, (p - 1) * face : p * face, :] = gl
                g = apply(mm_edge(c, order[c, 0, p]), gh, gl)
        TT[c] = g
    t_copy = remote(TT, TP, t_s, t_r, partner)
    t_copy.start()

    loads["prev0"].wait()
    for j in range(rows):
        LAT[0, 1, j] = prev_trace(0, j).astype(BF16)
        LAT[1, 1, j] = jnp.zeros((face, 256), BF16)
    loads["inlet"].wait()
    loads["upt"].wait()
    loads["aff"].wait()
    for c in range(cols):
        piece = jnp.where(is0, inlet[c, :, 0:half], inlet[c, :, half:])
        piece = jnp.where(zhi == 0, piece, jnp.zeros_like(piece))
        for it in range(2):
            OC[it, c, YS] = piece

    rate = upt[...].reshape(1, 256)
    affinity = aff[...].reshape(1, 256)

    inv_rate = 1.0 / rate
    ratio = affinity * inv_rate

    def source_of(x):
        return x / (inv_rate + ratio * jnp.abs(x))

    def put_source(c, j, x):
        hi, lo = split(source_of(x))
        SRC[c, 0, j] = hi
        SRC[c, 1, j] = lo
        a = A[c, j, edge:, :]
        F[c, j, edge:, :] = dot(a, hi) + dot(a, lo)

    def first_source(c):
        for j in range(rows):
            put_source(c, j, PV[c, j].astype(F32))

    def rest(c, js):
        for j in js:
            a = A[c, j, 0:edge, :]
            side_part = apply(NN[c, j, 0:edge, :], LAT[0, c, j], LAT[1, c, j])
            F[c, j, 0:edge, :] = dot(a, SRC[c, 0, j]) + dot(a, SRC[c, 1, j]) + side_part

    def maps_rest(c):
        for j in range(rows):
            put_maps(c, j, slice(0, edge))
            if c == 1:
                parts = [MM[c, j, a * 64 + 48 : a * 64 + 64, :].astype(F32)[8:16] for a in range(8)]
                MT[j] = cat0(*parts).astype(BF16)

    zero_trace = jnp.zeros((face, 256), BF16)

    def s1_copy(it, c):
        return remote(OS.at[it, c, 1 - core], OR.at[it, c], s1_s.at[it, c], s1_r.at[it, c], partner)

    def chain(it, c):
        for j in range(rows):
            F[c, j, edge:, :] += apply(NN[c, j, edge:, :], LAT[0, c, j], LAT[1, c, j])
        h = F[c, order[c, 0, 0], edge:, :]
        for p in range(1, rows):
            H[c, p - 1] = h
            hh, hl = split(h)
            j = order[c, 0, p]
            h = F[c, j, edge:, :] + apply(mm_edge(c, j), hh, hl)
        OS[it, c, 0] = h[:, 0:half]
        OS[it, c, 1] = h[:, half:]
        s1_copy(it, c).start()

    def first_second(it, c):
        own, got = OS[it, c, core], OR[it, c]
        return jnp.where(is0, own, got), jnp.where(is0, got, own)

    def s2_copy(it, c, d):
        return remote(OC.at[it, c, y], OC.at[it, c, y], s2_s.at[it, c, d - 1], s2_r.at[it, c, y], ypeer(d))

    def s2_arrival(it, c, d):
        source = lax.rem(y + d, YS)
        return remote(OC.at[it, c, source], OC.at[it, c, source], s2_s.at[it, c, d - 1], s2_r.at[it, c, source], ypeer(d))

    def compose(it, c):
        s1_copy(it, c).wait_recv()
        o_first, o_second = first_second(it, c)
        OC[it, c, y] = dot3(THL[1, c, 0], THL[1, c, 1], o_first) + o_second
        for d in (2, 1, 3):
            s2_copy(it, c, d).start()

    def z_copy(it, c):
        return remote(X8S.at[it, c], X8R.at[it, c], z_s.at[it, c], z_r.at[it, c], zpeer)

    def s4_copy(it, c):
        return remote(YSND.at[it, c], XIN.at[it, c, core], s4_s.at[it, c], s4_r.at[it, c], partner)

    def s4_arrival(it, c):
        return remote(YSND.at[it, c], XIN.at[it, c, 1 - core], s4_s.at[it, c], s4_r.at[it, c], partner)

    def put_entering(it, c, q):
        YSND[it, c] = jnp.where(is0, q[face:], q[0:face])
        XIN[it, c, core] = jnp.where(is0, q[0:face], q[face:])

    def gather(it, c):
        for d in (1, 3, 2):
            s2_arrival(it, c, d).wait_recv()
        offsets = OC[it, c].reshape((YS + 1) * face, half)
        q = dot3(VV[c, 0], VV[c, 1], offsets)
        o_first, _ = first_second(it, c)
        q = cat0(q[0:face], q[face : 2 * face] + o_first, q[2 * face :])

        @pl.when(zhi == 0)
        def _():
            X8S[it, c] = q[2 * face :]
            z_copy(it, c).start()
            put_entering(it, c, q[0 : 2 * face])
            s4_copy(it, c).start()

        @pl.when(zhi == 1)
        def _():
            X8S[it, c] = q[0:face]
            YSND[it, c] = q[face : 2 * face]

    def carry(it, c):
        @pl.when(zhi == 1)
        def _():
            z_copy(it, c).wait_recv()
            q = cat0(X8S[it, c], YSND[it, c])
            v = slice(YS * face, (YS + 1) * face)
            q = q + dot3(VV[c, 0, 0 : 2 * face, v], VV[c, 1, 0 : 2 * face, v], X8R[it, c])
            put_entering(it, c, q)
            s4_copy(it, c).start()

    def inflows(it, c):
        s4_arrival(it, c).wait_recv()
        x = jnp.concatenate([XIN[it, c, 0], XIN[it, c, 1]], axis=1)
        xh, xl = split(x)
        INF[0, c, 0] = xh
        INF[1, c, 0] = xl
        later = dot(G[c, 0], xh) + (dot(G[c, 1], xh) + dot(G[c, 0], xl))
        for p in range(1, rows):
            xh, xl = split(later[(p - 1) * face : p * face] + H[c, p - 1])
            INF[0, c, p] = xh
            INF[1, c, p] = xl

    def rank_of(c, j):
        rank = jnp.int32(0)
        for p in range(1, rows):
            rank = jnp.where(order[c, 0, p] == j, p, rank)
        return rank

    def solved(c, j):
        rank = rank_of(c, j)
        return F[c, j] + apply(MM[c, j], INF[0, c, rank], INF[1, c, rank])

    def traces_ahead():
        for j in range(rows):
            rank = rank_of(1, j)
            base = cat0(*[F[1, j, a * 64 + 56 : a * 64 + 64, :] for a in range(8)])
            LS[1, j] = base + apply(MT[j], INF[0, 1, rank], INF[1, 1, rank])

    def lag(c):
        for j in range(rows):
            x = solved(c, j)
            if c == 0:
                hi, lo = split(value_trace(x))
                LAT[0, 1, j] = hi
                LAT[1, 1, j] = lo
            put_source(c, j, x)

    def finish(c):
        for j in range(rows):
            out[c, 0, j] = solved(c, j).astype(BF16)

    def lat_arrival(it):
        @pl.when(lat > 0)
        def _():
            lat_copy(it).wait_recv()
            for j in range(rows):
                hi, lo = split(LR[it, j])
                LAT[0, 0, j] = hi
                LAT[1, 0, j] = lo

        @pl.when(lat == 0)
        def _():
            for j in range(rows):
                LAT[0, 0, j] = zero_trace
                LAT[1, 0, j] = zero_trace

    first_source(1)

    t_copy.wait_recv()
    for c in range(cols):
        own, got = TT[c], TP[c]
        t0h, t0l = split(jnp.where(is0, own, got))
        t1h, t1l = split(jnp.where(is0, got, own))
        THL[0, c, 0], THL[0, c, 1], THL[1, c, 0], THL[1, c, 1] = t0h, t0l, t1h, t1l
        TC[y, c] = dot3(t1h, t1l, jnp.where(is0, own, got))

    def tc_copy(d):
        return remote(TC.at[y], TC.at[y], tc_s.at[d - 1], tc_r.at[y], ypeer(d))

    def tc_arrival(d):
        source = lax.rem(y + d, YS)
        return remote(TC.at[source], TC.at[source], tc_s.at[d - 1], tc_r.at[source], ypeer(d))

    for d in (2, 1, 3):
        tc_copy(d).start()

    chain(0, 1)
    first_source(0)
    compose(0, 1)
    loads["ar1"].wait()
    maps_rest(1)

    for d in (1, 3, 2):
        tc_arrival(d).wait_recv()
    width = (YS + 1) * face
    row_id = lax.broadcasted_iota(jnp.int32, (face, width), 0)
    lane_id = lax.broadcasted_iota(jnp.int32, (face, width), 1)

    def unit(block):
        return jnp.where(lane_id - face * block == row_id, 1.0, 0.0).astype(F32)

    for c in range(cols):
        x = unit(YS)
        mine = jnp.where(y == 0, x, jnp.zeros_like(x))
        for t in range(YS):
            if t == 0:
                x = cat_lanes(TC[0, c], width) + unit(0)
            else:
                th, tl = split(TC[t, c])
                x = dot3(th, tl, x) + unit(t)
            if t + 1 < YS:
                mine = jnp.where(y == t + 1, x, mine)
        both = dot3(THL[0, c, 0], THL[0, c, 1], mine)
        vh, vl = split(cat0(mine, both, x))
        VV[c, 0] = vh
        VV[c, 1] = vl

    early, late = range(0, 2), range(2, rows)
    lat_arrival(0)
    chain(0, 0)
    gather(0, 1)
    rest(1, early)
    compose(0, 0)
    rest(1, late)
    loads["ar0"].wait()
    maps_rest(0)
    rest(0, range(rows))
    gather(0, 0)
    carry(0, 1)
    inflows(0, 1)
    traces_ahead()
    lat_send(1)
    lag(1)
    carry(0, 0)
    inflows(0, 0)
    lag(0)

    chain(1, 1)
    lat_arrival(1)
    chain(1, 0)
    rest(1, early)
    compose(1, 1)
    compose(1, 0)
    rest(1, late)
    rest(0, range(rows))

    def sent(it):
        for c in range(cols):
            s1_copy(it, c).wait_send()
            s4_copy(it, c).wait_send()
            for d in range(1, YS):
                s2_copy(it, c, d).wait_send()

        @pl.when(zhi == 0)
        def _():
            for c in range(cols):
                z_copy(it, c).wait_send()

        @pl.when(lat < lats - 1)
        def _():
            lat_copy(it).wait_send()

    t_copy.wait_send()
    for d in range(1, YS):
        tc_copy(d).wait_send()
    sent(0)
    gather(1, 1)
    carry(1, 1)
    gather(1, 0)
    carry(1, 0)
    inflows(1, 1)
    finish(1)
    inflows(1, 0)
    finish(0)
    sent(1)


def cat_lanes(t, width):
    face = t.shape[0]
    return jnp.concatenate([jnp.zeros((face, width - face), F32), t], axis=1)


def per_device(inverse, upwind, lateral, inlet_trace, previous, uptake_rate, affinity, flow_order):
    operands = (flow_order, inverse, upwind, lateral, inlet_trace, previous, uptake_rate, affinity)
    hbm = pl.BlockSpec(memory_space=pltpu.HBM)
    vmem = pl.BlockSpec(memory_space=pltpu.VMEM)
    dma = pltpu.SemaphoreType.DMA
    scratch = [
        pltpu.SMEM((2, 1, 4), jnp.int32),
        pltpu.VMEM((2, 64, 256), F32),
        pltpu.VMEM((256,), F32),
        pltpu.VMEM((256,), F32),
        pltpu.VMEM((2, 4, 512, 512), BF16),
        pltpu.VMEM((2, 4, 256, 512), BF16),
        pltpu.VMEM((2, 4, 512, 256), BF16),
        pltpu.VMEM((2, 4, 512, 256), BF16),
        pltpu.VMEM((2, 4, 512, 256), BF16),
        pltpu.VMEM((4, 64, 256), BF16),
        pltpu.VMEM((2, 4, 512, 256), F32),
        pltpu.VMEM((2, 2, 4, 512, 256), BF16),
        pltpu.VMEM((2, 4, 64, 256), F32),
        pltpu.VMEM((2, 4, 64, 256), F32),
        pltpu.VMEM((2, 2, 4, 64, 256), BF16),
        pltpu.VMEM((2, 3, 64, 256), F32),
        pltpu.VMEM((2, 2, 192, 64), BF16),
        pltpu.VMEM((2, 2, 4, 64, 256), BF16),
        pltpu.VMEM((2, 64, 64), F32),
        pltpu.VMEM((2, 64, 64), F32),
        pltpu.VMEM((4, 2, 64, 64), F32),
        pltpu.VMEM((2, 2, 2, 64, 64), BF16),
        pltpu.VMEM((2, 2, 192, 320), BF16),
        pltpu.VMEM((2, 2, 2, 64, 128), F32),
        pltpu.VMEM((2, 2, 64, 128), F32),
        pltpu.VMEM((2, 2, 5, 64, 128), F32),
        pltpu.VMEM((2, 2, 64, 128), F32),
        pltpu.VMEM((2, 2, 64, 128), F32),
        pltpu.VMEM((2, 2, 64, 128), F32),
        pltpu.VMEM((2, 2, 2, 64, 128), F32),
        dma((18,)),
        dma((2,)), dma((2,)),
        dma, dma,
        dma((3,)), dma((4,)),
        dma((2, 2)), dma((2, 2)),
        dma((2, 2, 3)), dma((2, 2, 4)),
        dma((2, 2)), dma((2, 2)),
        dma((2, 2)), dma((2, 2)),
    ]
    return pl.pallas_call(
        kernel,
        out_shape=jax.ShapeDtypeStruct(previous.shape, BF16),
        in_specs=[hbm] * 8,
        out_specs=vmem,
        scratch_shapes=scratch,
        compiler_params=pltpu.CompilerParams(
            collective_id=0, has_side_effects=True, vmem_limit_bytes=40 * 1024 * 1024
        ),
    )(*(pltpu.with_memory_space_constraint(a, pltpu.HBM) for a in operands))


def solution(mesh):
    placed = (
        P("lat", "stream", None, None, None),
        P("lat", "stream", None, None, None),
        P("lat", "stream", None, None, None),
        P("lat", None, None),
        P("lat", "stream", None, None, None),
        P(),
        P(),
        P("lat", "stream", None),
    )
    return jax.shard_map(
        per_device,
        mesh=mesh,
        in_specs=placed,
        out_specs=P("lat", "stream", None, None, None),
        check_vma=False,
    )
```

```python
import functools

import jax
import jax.numpy as jnp
from jax import lax
from jax.experimental import pallas as pl
from jax.experimental.pallas import tpu as pltpu
from jax.sharding import PartitionSpec as P

MESH = pl.DeviceIdType.MESH
F32 = jnp.float32
BF16 = jnp.bfloat16
YS = 4


def split(x):
    hi = x.astype(BF16)
    return hi, (x - hi.astype(F32)).astype(BF16)


def dot(a, b):
    return jnp.dot(a, b, preferred_element_type=F32)


def dot_nt(a, b):
    return lax.dot_general(a, b, (((1,), (1,)), ((), ())), preferred_element_type=F32)


def dot3(ah, al, b):
    bh, bl = split(b)
    return dot(ah, bh) + (dot(al, bh) + dot(ah, bl))


def cat0(*xs):
    return jnp.concatenate(xs, axis=0)


def kernel(
    order_in, inv, up, side, inlet_in, prev, upt_in, aff_in, out,
    order, inlet, upt, aff, A, UL, PV, MM, NN, F, SRC, LS, LR, LAT, H, G, INF, TT, TP, TC, THL, VV,
    OS, OR, OC, X8S, X8R, YSND, XIN, VO, XE, XL, RS, RR,
    ld_sem, lat_s, lat_r, t_s, t_r, tc_s, tc_r, s1_s, s1_r, s2_s, s2_r, z_s, z_r, s4_s, s4_r, x_s, x_r, r_s, r_r, ready,
):
    cols, rows, nodes, face = 2, 4, 512, 64
    half = 128
    edge = nodes - face
    s = lax.axis_index("stream")
    lat = lax.axis_index("lat")
    lats = lax.axis_size("lat")
    core = lax.rem(s, 2)
    y = lax.rem(s // 2, YS)
    zhi = s // (2 * YS)
    is0 = core == 0
    partner = {"stream": s + 1 - 2 * core}

    def ypeer(d):
        return {"stream": zhi * (2 * YS) + lax.rem(y + d, YS) * 2 + core}


    def above(k):
        return {"stream": 2 * YS + 2 * y + k}

    def below(k):
        return {"stream": 2 * y + k}

    loads = {}

    def load(name, k, src, dst):
        c = pltpu.make_async_copy(src, dst, ld_sem.at[k])
        c.start()
        loads[name] = c

    load("prev1", 0, prev.at[1, 0], PV.at[1])
    for c in (1, 0):
        for k in range(2):
            load(f"u{c}{k}", 2 + 2 * c + k, up.at[c, 0], UL.at[c, :, k * face : (k + 1) * face])
            load(f"l{c}{k}", 6 + 2 * c + k, side.at[c, 0], UL.at[c, :, (2 + k) * face : (3 + k) * face])
        load(f"al{c}", 10 + c, inv.at[c, 0, :, edge:], A.at[c, :, edge:])
        if c:
            load("order", 14, order_in, order)
            load("upt", 15, upt_in, upt)
            load("aff", 16, aff_in, aff)
    load("prev0", 1, prev.at[0, 0], PV.at[0])
    load("inlet", 17, inlet_in, inlet)
    load("ar1", 13, inv.at[1, 0, :, 0:edge], A.at[1, :, 0:edge])
    load("ar0", 12, inv.at[0, 0, :, 0:edge], A.at[0, :, 0:edge])

    barrier = pltpu.get_barrier_semaphore()

    def hello(peer):
        pl.semaphore_signal(barrier, inc=1, device_id=peer, device_id_type=MESH)

    for peer in (partner, ypeer(1), ypeer(2), ypeer(3)):
        hello(peer)

    @pl.when(lat > 0)
    def _():
        hello({"lat": lat - 1})

    @pl.when(zhi == 0)
    def _():
        hello(above(0))
        hello(above(1))

    expected = 4 + jnp.where(lat < lats - 1, 1, 0) + jnp.where(zhi == 1, 2, 0)

    def remote(src, dst, ssem, rsem, peer):
        return pltpu.make_async_remote_copy(
            src_ref=src, dst_ref=dst, send_sem=ssem, recv_sem=rsem, device_id=peer, device_id_type=MESH
        )

    def lat_copy(it):
        return remote(LS.at[it], LR.at[it], lat_s.at[it], lat_r.at[it], {"lat": lax.rem(lat + 1, lats)})

    def lat_send(it):
        @pl.when(lat < lats - 1)
        def _():
            lat_copy(it).start()

    def prev_trace(c, j):
        parts = []
        for a in range(8):
            piece = PV[c, j, a * 64 + 48 : a * 64 + 64, :].astype(F32)
            parts.append(piece[8:16])
        return cat0(*parts)

    def value_trace(x):
        return cat0(*[x[a * 64 + 56 : a * 64 + 64] for a in range(8)])

    def apply(m4, h, l):
        return dot(m4, cat0(h, l, h, l))

    def put_maps(c, j, rows_of):
        hi, lo = split(dot_nt(A[c, j, rows_of, :], UL[c, j]))
        MM[c, j, rows_of, 0:128] = hi[:, 0:128]
        MM[c, j, rows_of, 128:256] = lo[:, 0:128]
        NN[c, j, rows_of, 0:128] = hi[:, 128:256]
        NN[c, j, rows_of, 128:256] = lo[:, 128:256]

    def edge_maps(c):
        for n in (f"u{c}0", f"u{c}1", f"l{c}0", f"l{c}1", f"al{c}"):
            loads[n].wait()
        for j in range(rows):
            put_maps(c, j, slice(edge, nodes))

    loads["prev1"].wait()
    for j in range(rows):
        LS[0, j] = prev_trace(1, j)
    pl.semaphore_wait(barrier, expected)
    lat_send(0)

    @pl.when(zhi == 1)
    def _():
        for k in range(2):
            pl.semaphore_signal(ready, inc=1, device_id=below(k), device_id_type=MESH)

    edge_maps(1)

    edge_maps(0)
    loads["order"].wait()

    def mm_edge(c, j):
        return MM[c, j, edge:, :]

    eye_row = lax.broadcasted_iota(jnp.int32, (face, face), 0)
    eye_lane = lax.broadcasted_iota(jnp.int32, (face, face), 1)
    eye = jnp.where(eye_row == eye_lane, 1.0, 0.0).astype(BF16)
    for c in range(cols):
        G[c, 0, 0] = eye
        G[c, 1, 0] = jnp.zeros((face, face), BF16)
        first = mm_edge(c, order[c, 0, 0])
        g = first[:, 0:face].astype(F32) + first[:, 128 : 128 + face].astype(F32)
        for p in range(1, rows + 1):
            if p < rows:
                gh, gl = split(g)
                G[c, 0, p] = gh
                G[c, 1, p] = gl
                g = apply(mm_edge(c, order[c, 0, p]), gh, gl)
        TT[c] = g
    t_copy = remote(TT, TP, t_s, t_r, partner)
    t_copy.start()

    loads["prev0"].wait()
    for j in range(rows):
        LAT[0, 1, j] = prev_trace(0, j).astype(BF16)
        LAT[1, 1, j] = jnp.zeros((face, 256), BF16)
    loads["inlet"].wait()
    loads["upt"].wait()
    loads["aff"].wait()
    for c in range(cols):
        piece = jnp.where(is0, inlet[c, :, 0:half], inlet[c, :, half:])
        piece = jnp.where(zhi == 0, piece, jnp.zeros_like(piece))
        for it in range(2):
            OC[it, c, YS] = piece

    rate = upt[...].reshape(1, 256)
    affinity = aff[...].reshape(1, 256)

    inv_rate = 1.0 / rate
    ratio = affinity * inv_rate

    def source_of(x):
        return x / (inv_rate + ratio * jnp.abs(x))

    def put_source(c, j, x):
        hi, lo = split(source_of(x))
        SRC[c, 0, j] = hi
        SRC[c, 1, j] = lo
        a = A[c, j, edge:, :]
        F[c, j, edge:, :] = dot(a, hi) + dot(a, lo)

    def first_source(c):
        for j in range(rows):
            put_source(c, j, PV[c, j].astype(F32))

    def rest(c, js):
        for j in js:
            a = A[c, j, 0:edge, :]
            side_part = apply(NN[c, j, 0:edge, :], LAT[0, c, j], LAT[1, c, j])
            F[c, j, 0:edge, :] = dot(a, SRC[c, 0, j]) + dot(a, SRC[c, 1, j]) + side_part

    def maps_rest(c):
        for j in range(rows):
            put_maps(c, j, slice(0, edge))

    zero_trace = jnp.zeros((face, 256), BF16)

    def s1_copy(it, c):
        return remote(OS.at[it, c, 1 - core], OR.at[it, c], s1_s.at[it, c], s1_r.at[it, c], partner)

    def chain(it, c):
        for j in range(rows):
            F[c, j, edge:, :] += apply(NN[c, j, edge:, :], LAT[0, c, j], LAT[1, c, j])
        h = F[c, order[c, 0, 0], edge:, :]
        for p in range(1, rows):
            H[c, p - 1] = h
            hh, hl = split(h)
            j = order[c, 0, p]
            h = F[c, j, edge:, :] + apply(mm_edge(c, j), hh, hl)
        OS[it, c, 0] = h[:, 0:half]
        OS[it, c, 1] = h[:, half:]
        s1_copy(it, c).start()

    def first_second(it, c):
        own, got = OS[it, c, core], OR[it, c]
        return jnp.where(is0, own, got), jnp.where(is0, got, own)

    def s2_copy(it, c, d):
        return remote(OC.at[it, c, y], OC.at[it, c, y], s2_s.at[it, c, d - 1], s2_r.at[it, c, y], ypeer(d))

    def s2_arrival(it, c, d):
        source = lax.rem(y + d, YS)
        return remote(OC.at[it, c, source], OC.at[it, c, source], s2_s.at[it, c, d - 1], s2_r.at[it, c, source], ypeer(d))

    def compose(it, c):
        s1_copy(it, c).wait_recv()
        o_first, o_second = first_second(it, c)
        OC[it, c, y] = dot3(THL[1, c, 0], THL[1, c, 1], o_first) + o_second
        for d in (2, 1, 3):
            s2_copy(it, c, d).start()

    def z_copy(it, c, k):
        return remote(X8S.at[it, c], X8R.at[it, c, core], z_s.at[it, c, k], z_r.at[it, c, core], above(k))

    def z_arrival(it, c, h):
        return remote(X8S.at[it, c], X8R.at[it, c, h], z_s.at[it, c, h], z_r.at[it, c, h], partner)

    def s4_copy(it, c):
        return remote(YSND.at[it, c], XIN.at[it, c, core], s4_s.at[it, c], s4_r.at[it, c], partner)

    def s4_arrival(it, c):
        return remote(YSND.at[it, c], XIN.at[it, c, 1 - core], s4_s.at[it, c], s4_r.at[it, c], partner)

    def gather(it, c):
        for d in (1, 3, 2):
            s2_arrival(it, c, d).wait_recv()
        offsets = OC[it, c].reshape((YS + 1) * face, half)
        q = dot3(VV[c, 0], VV[c, 1], offsets)
        o_first, _ = first_second(it, c)
        first, second = q[0:face], q[face : 2 * face] + o_first

        @pl.when(zhi == 0)
        def _():
            X8S[it, c] = q[2 * face :]
            if it == 0 and c == 1:
                pl.semaphore_wait(ready, 2)
            for k in range(2):
                z_copy(it, c, k).start()

        YSND[it, c] = jnp.where(is0, second, first)
        XIN[it, c, core] = jnp.where(is0, first, second)
        s4_copy(it, c).start()

    def x_copy():
        return remote(XE.at[0, 1], XL, x_s, x_r, {"lat": lax.rem(lat + 1, lats)})

    def r_copy():
        return remote(RS, RR, r_s, r_r, {"lat": lax.rem(lat + 1, lats)})

    def enter(it, c):
        s4_arrival(it, c).wait_recv()
        XE[it, c] = jnp.concatenate([XIN[it, c, 0], XIN[it, c, 1]], axis=1)

        @pl.when(zhi == 1)
        def _():
            for h in range(2):
                z_arrival(it, c, h).wait_recv()
            carried = jnp.concatenate([X8R[it, c, 0], X8R[it, c, 1]], axis=1)
            XE[it, c] += dot3(VO[c, 0], VO[c, 1], carried)

        if it == 0 and c == 1:

            @pl.when(lat < lats - 1)
            def _():
                x_copy().start()

    def inflows(it, c):
        xh, xl = split(XE[it, c])
        INF[0, c, 0] = xh
        INF[1, c, 0] = xl
        gh = G[c, 0, 1:].reshape((rows - 1) * face, face)
        gl = G[c, 1, 1:].reshape((rows - 1) * face, face)
        later = dot(gh, xh) + (dot(gl, xh) + dot(gh, xl))
        for p in range(1, rows):
            xh, xl = split(later[(p - 1) * face : p * face] + H[c, p - 1])
            INF[0, c, p] = xh
            INF[1, c, p] = xl

    def rank_of(c, j):
        rank = jnp.int32(0)
        for p in range(1, rows):
            rank = jnp.where(order[c, 0, p] == j, p, rank)
        return rank

    def solved(c, j):
        rank = rank_of(c, j)
        return F[c, j] + apply(MM[c, j], INF[0, c, rank], INF[1, c, rank])

    def traces_ahead():
        for j in range(rows):
            a = cat0(*[A[1, j, i * 64 + 48 : i * 64 + 64, :].astype(F32)[8:16] for i in range(8)]).astype(BF16)
            hi, lo = split(dot_nt(a, UL[1, j]))
            mt = jnp.concatenate([hi[:, 0:128], lo[:, 0:128]], axis=1)
            nt = jnp.concatenate([hi[:, 128:256], lo[:, 128:256]], axis=1)
            rank = rank_of(1, j)
            hh, hl = split(jnp.where(rank > 0, H[1, jnp.maximum(rank - 1, 0)], 0.0))
            base = dot(a, SRC[1, 0, j]) + dot(a, SRC[1, 1, j])
            LS[1, j] = base + apply(nt, LAT[0, 1, j], LAT[1, 1, j]) + apply(mt, hh, hl)
            RS[j] = apply(mt, G[1, 0, rank], G[1, 1, rank])

        @pl.when(lat < lats - 1)
        def _():
            r_copy().start()
            lat_copy(1).start()

    def lag(c):
        for j in range(rows):
            x = solved(c, j)
            if c == 0:
                hi, lo = split(value_trace(x))
                LAT[0, 1, j] = hi
                LAT[1, 1, j] = lo
            put_source(c, j, x)

    def finish(c):
        for j in range(rows):
            out[c, 0, j] = solved(c, j).astype(BF16)

    def lat_arrival(it):
        @pl.when(lat > 0)
        def _():
            lat_copy(it).wait_recv()
            if it == 1:
                r_copy().wait_recv()
                x_copy().wait_recv()
                xh, xl = split(XL[...])
            for j in range(rows):
                trace = LR[it, j]
                if it == 1:
                    rh, rl = split(RR[j])
                    trace = trace + (dot(rh, xh) + (dot(rl, xh) + dot(rh, xl)))
                hi, lo = split(trace)
                LAT[0, 0, j] = hi
                LAT[1, 0, j] = lo

        @pl.when(lat == 0)
        def _():
            for j in range(rows):
                LAT[0, 0, j] = zero_trace
                LAT[1, 0, j] = zero_trace

    def prefix_maps():
        for d in (1, 3, 2):
            tc_arrival(d).wait_recv()
        width = (YS + 1) * face
        row_id = lax.broadcasted_iota(jnp.int32, (face, width), 0)
        lane_id = lax.broadcasted_iota(jnp.int32, (face, width), 1)

        def unit(block):
            return jnp.where(lane_id - face * block == row_id, 1.0, 0.0).astype(F32)

        for c in range(cols):
            x = unit(YS)
            mine = jnp.where(y == 0, x, jnp.zeros_like(x))
            for t in range(YS):
                if t == 0:
                    x = cat_lanes(TC[0, c], width) + unit(0)
                else:
                    th, tl = split(TC[t, c])
                    x = dot3(th, tl, x) + unit(t)
                if t + 1 < YS:
                    mine = jnp.where(y == t + 1, x, mine)
            both = dot3(THL[0, c, 0], THL[0, c, 1], mine)
            vh, vl = split(cat0(mine, both, x))
            VV[c, 0] = vh
            VV[c, 1] = vl
            v = slice(YS * face, (YS + 1) * face)
            VO[c, 0] = jnp.where(is0, vh[0:face, v], vh[face : 2 * face, v])
            VO[c, 1] = jnp.where(is0, vl[0:face, v], vl[face : 2 * face, v])

    first_source(1)

    t_copy.wait_recv()
    for c in range(cols):
        own, got = TT[c], TP[c]
        t0h, t0l = split(jnp.where(is0, own, got))
        t1h, t1l = split(jnp.where(is0, got, own))
        THL[0, c, 0], THL[0, c, 1], THL[1, c, 0], THL[1, c, 1] = t0h, t0l, t1h, t1l
        TC[y, c] = dot3(t1h, t1l, jnp.where(is0, own, got))

    def tc_copy(d):
        return remote(TC.at[y], TC.at[y], tc_s.at[d - 1], tc_r.at[y], ypeer(d))

    def tc_arrival(d):
        source = lax.rem(y + d, YS)
        return remote(TC.at[source], TC.at[source], tc_s.at[d - 1], tc_r.at[source], ypeer(d))

    for d in (2, 1, 3):
        tc_copy(d).start()

    chain(0, 1)
    first_source(0)
    compose(0, 1)
    loads["ar1"].wait()
    traces_ahead()
    maps_rest(1)

    early, late = range(0, 2), range(2, rows)
    lat_arrival(0)
    chain(0, 0)
    rest(1, early)
    compose(0, 0)
    prefix_maps()
    gather(0, 1)
    rest(1, late)

    @pl.when(zhi == 0)
    def _():
        enter(0, 1)

    loads["ar0"].wait()
    maps_rest(0)
    rest(0, early)
    gather(0, 0)
    rest(0, late)

    @pl.when(zhi == 1)
    def _():
        enter(0, 1)

    inflows(0, 1)
    lag(1)
    enter(0, 0)
    inflows(0, 0)
    lag(0)
    lat_arrival(1)

    chain(1, 0)
    chain(1, 1)
    rest(0, range(0, 1))
    compose(1, 0)
    rest(0, range(1, 2))
    compose(1, 1)
    rest(0, late)
    rest(1, range(rows))

    def sent(it):
        for c in range(cols):
            s1_copy(it, c).wait_send()
            s4_copy(it, c).wait_send()
            for d in range(1, YS):
                s2_copy(it, c, d).wait_send()

        @pl.when(zhi == 0)
        def _():
            for c in range(cols):
                for k in range(2):
                    z_copy(it, c, k).wait_send()

        @pl.when(lat < lats - 1)
        def _():
            lat_copy(it).wait_send()

    t_copy.wait_send()
    for d in range(1, YS):
        tc_copy(d).wait_send()

    @pl.when(lat < lats - 1)
    def _():
        x_copy().wait_send()
        r_copy().wait_send()

    sent(0)
    gather(1, 0)
    gather(1, 1)
    enter(1, 0)
    inflows(1, 0)
    finish(0)
    enter(1, 1)
    inflows(1, 1)
    finish(1)
    sent(1)


def cat_lanes(t, width):
    face = t.shape[0]
    return jnp.concatenate([jnp.zeros((face, width - face), F32), t], axis=1)


def per_device(inverse, upwind, lateral, inlet_trace, previous, uptake_rate, affinity, flow_order):
    operands = (flow_order, inverse, upwind, lateral, inlet_trace, previous, uptake_rate, affinity)
    hbm = pl.BlockSpec(memory_space=pltpu.HBM)
    vmem = pl.BlockSpec(memory_space=pltpu.VMEM)
    dma = pltpu.SemaphoreType.DMA
    scratch = [
        pltpu.SMEM((2, 1, 4), jnp.int32),
        pltpu.VMEM((2, 64, 256), F32),
        pltpu.VMEM((256,), F32),
        pltpu.VMEM((256,), F32),
        pltpu.VMEM((2, 4, 512, 512), BF16),
        pltpu.VMEM((2, 4, 256, 512), BF16),
        pltpu.VMEM((2, 4, 512, 256), BF16),
        pltpu.VMEM((2, 4, 512, 256), BF16),
        pltpu.VMEM((2, 4, 512, 256), BF16),
        pltpu.VMEM((2, 4, 512, 256), F32),
        pltpu.VMEM((2, 2, 4, 512, 256), BF16),
        pltpu.VMEM((2, 4, 64, 256), F32),
        pltpu.VMEM((2, 4, 64, 256), F32),
        pltpu.VMEM((2, 2, 4, 64, 256), BF16),
        pltpu.VMEM((2, 3, 64, 256), F32),
        pltpu.VMEM((2, 2, 4, 64, 64), BF16),
        pltpu.VMEM((2, 2, 4, 64, 256), BF16),
        pltpu.VMEM((2, 64, 64), F32),
        pltpu.VMEM((2, 64, 64), F32),
        pltpu.VMEM((4, 2, 64, 64), F32),
        pltpu.VMEM((2, 2, 2, 64, 64), BF16),
        pltpu.VMEM((2, 2, 192, 320), BF16),
        pltpu.VMEM((2, 2, 2, 64, 128), F32),
        pltpu.VMEM((2, 2, 64, 128), F32),
        pltpu.VMEM((2, 2, 5, 64, 128), F32),
        pltpu.VMEM((2, 2, 64, 128), F32),
        pltpu.VMEM((2, 2, 2, 64, 128), F32),
        pltpu.VMEM((2, 2, 64, 128), F32),
        pltpu.VMEM((2, 2, 2, 64, 128), F32),
        pltpu.VMEM((2, 2, 64, 64), BF16),
        pltpu.VMEM((2, 2, 64, 256), F32),
        pltpu.VMEM((64, 256), F32),
        pltpu.VMEM((4, 64, 64), F32),
        pltpu.VMEM((4, 64, 64), F32),
        dma((18,)),
        dma((2,)), dma((2,)),
        dma, dma,
        dma((3,)), dma((4,)),
        dma((2, 2)), dma((2, 2)),
        dma((2, 2, 3)), dma((2, 2, 4)),
        dma((2, 2, 2)), dma((2, 2, 2)),
        dma((2, 2)), dma((2, 2)),
        dma, dma, dma, dma,
        pltpu.SemaphoreType.REGULAR,
    ]
    return pl.pallas_call(
        kernel,
        out_shape=jax.ShapeDtypeStruct(previous.shape, BF16),
        in_specs=[hbm] * 8,
        out_specs=vmem,
        scratch_shapes=scratch,
        compiler_params=pltpu.CompilerParams(
            collective_id=0, has_side_effects=True, vmem_limit_bytes=40 * 1024 * 1024
        ),
    )(*(pltpu.with_memory_space_constraint(a, pltpu.HBM) for a in operands))


def solution(mesh):
    placed = (
        P("lat", "stream", None, None, None),
        P("lat", "stream", None, None, None),
        P("lat", "stream", None, None, None),
        P("lat", None, None),
        P("lat", "stream", None, None, None),
        P(),
        P(),
        P("lat", "stream", None),
    )
    return jax.shard_map(
        per_device,
        mesh=mesh,
        in_specs=placed,
        out_specs=P("lat", "stream", None, None, None),
        check_vma=False,
    )
```

```python
import functools

import jax
import jax.numpy as jnp
from jax import lax
from jax.experimental import pallas as pl
from jax.experimental.pallas import tpu as pltpu
from jax.sharding import PartitionSpec as P

MESH = pl.DeviceIdType.MESH
F32 = jnp.float32
BF16 = jnp.bfloat16
YS = 4


def split(x):
    hi = x.astype(BF16)
    return hi, (x - hi.astype(F32)).astype(BF16)


def dot(a, b):
    return jnp.dot(a, b, preferred_element_type=F32)


def dot_nt(a, b):
    return lax.dot_general(a, b, (((1,), (1,)), ((), ())), preferred_element_type=F32)


def dot3(ah, al, b):
    bh, bl = split(b)
    return dot(ah, bh) + (dot(al, bh) + dot(ah, bl))


def cat0(*xs):
    return jnp.concatenate(xs, axis=0)


def kernel(
    order_in, inv, up, side, inlet_in, prev, upt_in, aff_in, out,
    order, inlet, upt, aff, A, UL, PV, MM, NN, F, SRC, LS, LR, LAT, H, G, INF, TT, TP, TC, THL, VV,
    OS, OR, OC, X8S, X8R, YSND, XIN, VO, XE, XL, RS, RR, RL,
    ld_sem, lat_s, lat_r, t_s, t_r, tc_s, tc_r, s1_s, s1_r, s2_s, s2_r, z_s, z_r, s4_s, s4_r, x_s, x_r, r_s, r_r, rl_s, rl_r, ready,
):
    cols, rows, nodes, face = 2, 4, 512, 64
    half = 128
    edge = nodes - face
    s = lax.axis_index("stream")
    lat = lax.axis_index("lat")
    lats = lax.axis_size("lat")
    core = lax.rem(s, 2)
    y = lax.rem(s // 2, YS)
    zhi = s // (2 * YS)
    is0 = core == 0
    xs = 4
    bends = (lax.rem(lat, xs) == xs - 1) & (lat < lats - 1)
    relays = (lax.rem(lat, xs) == 0) & (lat < lats - xs)
    relayed = (lax.rem(lat, xs) == 0) & (lat > 0)
    partner = {"stream": s + 1 - 2 * core}

    def ypeer(d):
        return {"stream": zhi * (2 * YS) + lax.rem(y + d, YS) * 2 + core}


    def above(k):
        return {"stream": 2 * YS + 2 * y + k}

    def below(k):
        return {"stream": 2 * y + k}

    barrier = pltpu.get_barrier_semaphore()

    def hello(peer):
        pl.semaphore_signal(barrier, inc=1, device_id=peer, device_id_type=MESH)

    for peer in (partner, ypeer(1), ypeer(2), ypeer(3)):
        hello(peer)

    @pl.when(lat > 0)
    def _():
        hello({"lat": lat - 1})

    @pl.when(relays)
    def _():
        hello({"lat": lat + xs - 1})

    @pl.when(relayed)
    def _():
        hello({"lat": lat - xs})

    @pl.when(zhi == 0)
    def _():
        hello(above(0))
        hello(above(1))

    expected = 4 + jnp.where(lat < lats - 1, 1, 0) + jnp.where(zhi == 1, 2, 0)
    expected = expected + jnp.where(bends, 1, 0) + jnp.where(relays, 1, 0)

    loads = {}

    def load(name, k, src, dst):
        c = pltpu.make_async_copy(src, dst, ld_sem.at[k])
        c.start()
        loads[name] = c

    load("prev1", 0, prev.at[1, 0], PV.at[1])
    for c in (1, 0):
        for k in range(2):
            load(f"u{c}{k}", 2 + 2 * c + k, up.at[c, 0], UL.at[c, :, k * face : (k + 1) * face])
            load(f"l{c}{k}", 6 + 2 * c + k, side.at[c, 0], UL.at[c, :, (2 + k) * face : (3 + k) * face])
        load(f"al{c}", 10 + c, inv.at[c, 0, :, edge:], A.at[c, :, edge:])
        if c:
            load("order", 14, order_in, order)
            load("upt", 15, upt_in, upt)
            load("aff", 16, aff_in, aff)
    load("prev0", 1, prev.at[0, 0], PV.at[0])
    load("inlet", 17, inlet_in, inlet)
    load("ar1", 13, inv.at[1, 0, :, 0:edge], A.at[1, :, 0:edge])
    load("ar0", 12, inv.at[0, 0, :, 0:edge], A.at[0, :, 0:edge])

    def remote(src, dst, ssem, rsem, peer):
        return pltpu.make_async_remote_copy(
            src_ref=src, dst_ref=dst, send_sem=ssem, recv_sem=rsem, device_id=peer, device_id_type=MESH
        )

    def lat_copy(it):
        return remote(LS.at[it], LR.at[it], lat_s.at[it], lat_r.at[it], {"lat": lax.rem(lat + 1, lats)})

    def lat_send(it):
        @pl.when(lat < lats - 1)
        def _():
            lat_copy(it).start()

    def prev_trace(c, j):
        parts = []
        for a in range(8):
            piece = PV[c, j, a * 64 + 48 : a * 64 + 64, :].astype(F32)
            parts.append(piece[8:16])
        return cat0(*parts)

    def value_trace(x):
        return cat0(*[x[a * 64 + 56 : a * 64 + 64] for a in range(8)])

    def apply(m4, h, l):
        return dot(m4, cat0(h, l, h, l))

    def put_maps(c, j, rows_of):
        hi, lo = split(dot_nt(A[c, j, rows_of, :], UL[c, j]))
        MM[c, j, rows_of, 0:128] = hi[:, 0:128]
        MM[c, j, rows_of, 128:256] = lo[:, 0:128]
        NN[c, j, rows_of, 0:128] = hi[:, 128:256]
        NN[c, j, rows_of, 128:256] = lo[:, 128:256]

    def edge_maps(c):
        for n in (f"u{c}0", f"u{c}1", f"l{c}0", f"l{c}1", f"al{c}"):
            loads[n].wait()
        for j in range(rows):
            put_maps(c, j, slice(edge, nodes))

    loads["prev1"].wait()
    for j in range(rows):
        LS[0, j] = prev_trace(1, j)
    pl.semaphore_wait(barrier, expected)
    lat_send(0)

    @pl.when(zhi == 1)
    def _():
        for k in range(2):
            pl.semaphore_signal(ready, inc=1, device_id=below(k), device_id_type=MESH)

    edge_maps(1)

    edge_maps(0)
    loads["order"].wait()

    def mm_edge(c, j):
        return MM[c, j, edge:, :]

    eye_row = lax.broadcasted_iota(jnp.int32, (face, face), 0)
    eye_lane = lax.broadcasted_iota(jnp.int32, (face, face), 1)
    eye = jnp.where(eye_row == eye_lane, 1.0, 0.0).astype(BF16)
    for c in range(cols):
        G[c, 0, 0] = eye
        G[c, 1, 0] = jnp.zeros((face, face), BF16)
        first = mm_edge(c, order[c, 0, 0])
        g = first[:, 0:face].astype(F32) + first[:, 128 : 128 + face].astype(F32)
        for p in range(1, rows + 1):
            if p < rows:
                gh, gl = split(g)
                G[c, 0, p] = gh
                G[c, 1, p] = gl
                g = apply(mm_edge(c, order[c, 0, p]), gh, gl)
        TT[c] = g
    t_copy = remote(TT, TP, t_s, t_r, partner)
    t_copy.start()

    loads["prev0"].wait()
    for j in range(rows):
        LAT[0, 1, j] = prev_trace(0, j).astype(BF16)
        LAT[1, 1, j] = jnp.zeros((face, 256), BF16)
    loads["inlet"].wait()
    loads["upt"].wait()
    loads["aff"].wait()
    for c in range(cols):
        piece = jnp.where(is0, inlet[c, :, 0:half], inlet[c, :, half:])
        piece = jnp.where(zhi == 0, piece, jnp.zeros_like(piece))
        for it in range(2):
            OC[it, c, YS] = piece

    rate = upt[...].reshape(1, 256)
    affinity = aff[...].reshape(1, 256)

    inv_rate = 1.0 / rate
    ratio = affinity * inv_rate

    def source_of(x):
        return x / (inv_rate + ratio * jnp.abs(x))

    def put_source(c, j, x):
        hi, lo = split(source_of(x))
        SRC[c, 0, j] = hi
        SRC[c, 1, j] = lo
        a = A[c, j, edge:, :]
        F[c, j, edge:, :] = dot(a, hi) + dot(a, lo)

    def first_source(c):
        for j in range(rows):
            put_source(c, j, PV[c, j].astype(F32))

    def rest(c, js):
        for j in js:
            a = A[c, j, 0:edge, :]
            side_part = apply(NN[c, j, 0:edge, :], LAT[0, c, j], LAT[1, c, j])
            F[c, j, 0:edge, :] = dot(a, SRC[c, 0, j]) + dot(a, SRC[c, 1, j]) + side_part

    def maps_rest(c):
        for j in range(rows):
            put_maps(c, j, slice(0, edge))

    zero_trace = jnp.zeros((face, 256), BF16)

    def s1_copy(it, c):
        return remote(OS.at[it, c, 1 - core], OR.at[it, c], s1_s.at[it, c], s1_r.at[it, c], partner)

    def chain(it, c):
        for j in range(rows):
            F[c, j, edge:, :] += apply(NN[c, j, edge:, :], LAT[0, c, j], LAT[1, c, j])
        h = F[c, order[c, 0, 0], edge:, :]
        for p in range(1, rows):
            H[c, p - 1] = h
            hh, hl = split(h)
            j = order[c, 0, p]
            h = F[c, j, edge:, :] + apply(mm_edge(c, j), hh, hl)
        OS[it, c, 0] = h[:, 0:half]
        OS[it, c, 1] = h[:, half:]
        s1_copy(it, c).start()

    def first_second(it, c):
        own, got = OS[it, c, core], OR[it, c]
        return jnp.where(is0, own, got), jnp.where(is0, got, own)

    def s2_copy(it, c, d):
        return remote(OC.at[it, c, y], OC.at[it, c, y], s2_s.at[it, c, d - 1], s2_r.at[it, c, y], ypeer(d))

    def s2_arrival(it, c, d):
        source = lax.rem(y + d, YS)
        return remote(OC.at[it, c, source], OC.at[it, c, source], s2_s.at[it, c, d - 1], s2_r.at[it, c, source], ypeer(d))

    def compose(it, c):
        s1_copy(it, c).wait_recv()
        o_first, o_second = first_second(it, c)
        OC[it, c, y] = dot3(THL[1, c, 0], THL[1, c, 1], o_first) + o_second
        for d in (2, 1, 3):
            s2_copy(it, c, d).start()

    def z_copy(it, c, k):
        return remote(X8S.at[it, c], X8R.at[it, c, core], z_s.at[it, c, k], z_r.at[it, c, core], above(k))

    def z_arrival(it, c, h):
        return remote(X8S.at[it, c], X8R.at[it, c, h], z_s.at[it, c, h], z_r.at[it, c, h], partner)

    def s4_copy(it, c):
        return remote(YSND.at[it, c], XIN.at[it, c, core], s4_s.at[it, c], s4_r.at[it, c], partner)

    def s4_arrival(it, c):
        return remote(YSND.at[it, c], XIN.at[it, c, 1 - core], s4_s.at[it, c], s4_r.at[it, c], partner)

    def gather(it, c):
        for d in (1, 3, 2):
            s2_arrival(it, c, d).wait_recv()
        offsets = OC[it, c].reshape((YS + 1) * face, half)
        q = dot3(VV[c, 0], VV[c, 1], offsets)
        o_first, _ = first_second(it, c)
        first, second = q[0:face], q[face : 2 * face] + o_first

        @pl.when(zhi == 0)
        def _():
            X8S[it, c] = q[2 * face :]
            if it == 0 and c == 1:
                pl.semaphore_wait(ready, 2)
            for k in range(2):
                z_copy(it, c, k).start()

        YSND[it, c] = jnp.where(is0, second, first)
        XIN[it, c, core] = jnp.where(is0, first, second)
        s4_copy(it, c).start()

    def x_copy():
        return remote(XE.at[0, 1], XL, x_s, x_r, {"lat": lax.rem(lat + 1, lats)})

    def r_copy():
        return remote(RS, RR, r_s, r_r, {"lat": lax.rem(lat + 1, lats)})

    def enter(it, c):
        s4_arrival(it, c).wait_recv()
        XE[it, c] = jnp.concatenate([XIN[it, c, 0], XIN[it, c, 1]], axis=1)

        @pl.when(zhi == 1)
        def _():
            for h in range(2):
                z_arrival(it, c, h).wait_recv()
            carried = jnp.concatenate([X8R[it, c, 0], X8R[it, c, 1]], axis=1)
            XE[it, c] += dot3(VO[c, 0], VO[c, 1], carried)

        if it == 0 and c == 1:

            @pl.when(lat < lats - 1)
            def _():
                x_copy().start()

    def inflows(it, c):
        xh, xl = split(XE[it, c])
        INF[0, c, 0] = xh
        INF[1, c, 0] = xl
        gh = G[c, 0, 1:].reshape((rows - 1) * face, face)
        gl = G[c, 1, 1:].reshape((rows - 1) * face, face)
        later = dot(gh, xh) + (dot(gl, xh) + dot(gh, xl))
        for p in range(1, rows):
            xh, xl = split(later[(p - 1) * face : p * face] + H[c, p - 1])
            INF[0, c, p] = xh
            INF[1, c, p] = xl

    def rank_of(c, j):
        rank = jnp.int32(0)
        for p in range(1, rows):
            rank = jnp.where(order[c, 0, p] == j, p, rank)
        return rank

    def solved(c, j):
        rank = rank_of(c, j)
        return F[c, j] + apply(MM[c, j], INF[0, c, rank], INF[1, c, rank])

    def traces_ahead():
        maps = []
        for j in range(rows):
            a = cat0(*[A[1, j, i * 64 + 48 : i * 64 + 64, :].astype(F32)[8:16] for i in range(8)]).astype(BF16)
            hi, lo = split(dot_nt(a, UL[1, j]))
            mt = jnp.concatenate([hi[:, 0:128], lo[:, 0:128]], axis=1)
            nt = jnp.concatenate([hi[:, 128:256], lo[:, 128:256]], axis=1)
            rank = rank_of(1, j)
            hh, hl = split(jnp.where(rank > 0, H[1, jnp.maximum(rank - 1, 0)], 0.0))
            base = dot(a, SRC[1, 0, j]) + dot(a, SRC[1, 1, j])
            LS[1, j] = base + apply(nt, LAT[0, 1, j], LAT[1, 1, j]) + apply(mt, hh, hl)
            maps.append(apply(mt, G[1, 0, rank], G[1, 1, rank]))
        for k in range(2):
            RS[k] = jnp.concatenate([maps[2 * k], maps[2 * k + 1]], axis=1)


        @pl.when(lat < lats - 1)
        def _():
            part_copy(0).start()

        @pl.when((lat < lats - 1) & jnp.logical_not(bends))
        def _():
            part_copy(1).start()
            r_copy().start()

        @pl.when(bends)
        def _():
            bend_copy().start()

    def map_send():
        @pl.when(bends)
        def _():
            r_copy().start()

    def part_copy(k):
        js = pl.ds(2 * k, 2)
        return remote(LS.at[1, js], LR.at[1, js], lat_s.at[1 + k], lat_r.at[1 + k], {"lat": lax.rem(lat + 1, lats)})

    back = pl.ds(2, 2)

    def bend_copy():
        peer = {"lat": lax.rem(lat + lats - xs + 1, lats)}
        return remote(LS.at[1, back], RL, lat_s.at[2], rl_r, peer)

    def relay_copy():
        peer = {"lat": lax.rem(lat + xs, lats)}
        return remote(RL, LR.at[1, back], rl_s, lat_r.at[2], peer)

    def pass_on():
        @pl.when(relays)
        def _():
            bend_copy().wait_recv()
            relay_copy().start()

    def lag(c):
        for j in range(rows):
            x = solved(c, j)
            if c == 0:
                hi, lo = split(value_trace(x))
                LAT[0, 1, j] = hi
                LAT[1, 1, j] = lo
            put_source(c, j, x)

    def finish(c):
        for j in range(rows):
            out[c, 0, j] = solved(c, j).astype(BF16)

    def lat_arrival(it):
        @pl.when(lat > 0)
        def _():
            if it == 0:
                lat_copy(it).wait_recv()
            else:
                for k in range(2):
                    part_copy(k).wait_recv()
                r_copy().wait_recv()
                x_copy().wait_recv()
                xh, xl = split(XL[...])
            for j in range(rows):
                trace = LR[it, j]
                if it == 1:
                    rh, rl = split(RR[j // 2][:, (j % 2) * face : (j % 2 + 1) * face])
                    trace = trace + (dot(rh, xh) + (dot(rl, xh) + dot(rh, xl)))
                hi, lo = split(trace)
                LAT[0, 0, j] = hi
                LAT[1, 0, j] = lo

        @pl.when(lat == 0)
        def _():
            for j in range(rows):
                LAT[0, 0, j] = zero_trace
                LAT[1, 0, j] = zero_trace

    def prefix_maps():
        for d in (1, 3, 2):
            tc_arrival(d).wait_recv()
        width = (YS + 1) * face
        row_id = lax.broadcasted_iota(jnp.int32, (face, width), 0)
        lane_id = lax.broadcasted_iota(jnp.int32, (face, width), 1)

        def unit(block):
            return jnp.where(lane_id - face * block == row_id, 1.0, 0.0).astype(F32)

        for c in range(cols):
            x = unit(YS)
            mine = jnp.where(y == 0, x, jnp.zeros_like(x))
            for t in range(YS):
                if t == 0:
                    x = cat_lanes(TC[0, c], width) + unit(0)
                else:
                    th, tl = split(TC[t, c])
                    x = dot3(th, tl, x) + unit(t)
                if t + 1 < YS:
                    mine = jnp.where(y == t + 1, x, mine)
            both = dot3(THL[0, c, 0], THL[0, c, 1], mine)
            vh, vl = split(cat0(mine, both, x))
            VV[c, 0] = vh
            VV[c, 1] = vl
            v = slice(YS * face, (YS + 1) * face)
            VO[c, 0] = jnp.where(is0, vh[0:face, v], vh[face : 2 * face, v])
            VO[c, 1] = jnp.where(is0, vl[0:face, v], vl[face : 2 * face, v])

    first_source(1)

    t_copy.wait_recv()
    for c in range(cols):
        own, got = TT[c], TP[c]
        t0h, t0l = split(jnp.where(is0, own, got))
        t1h, t1l = split(jnp.where(is0, got, own))
        THL[0, c, 0], THL[0, c, 1], THL[1, c, 0], THL[1, c, 1] = t0h, t0l, t1h, t1l
        TC[y, c] = dot3(t1h, t1l, jnp.where(is0, own, got))

    def tc_copy(d):
        return remote(TC.at[y], TC.at[y], tc_s.at[d - 1], tc_r.at[y], ypeer(d))

    def tc_arrival(d):
        source = lax.rem(y + d, YS)
        return remote(TC.at[source], TC.at[source], tc_s.at[d - 1], tc_r.at[source], ypeer(d))

    for d in (2, 1, 3):
        tc_copy(d).start()

    chain(0, 1)
    first_source(0)
    compose(0, 1)
    loads["ar1"].wait()
    traces_ahead()
    maps_rest(1)

    early, late = range(0, 2), range(2, rows)
    lat_arrival(0)
    chain(0, 0)
    rest(1, early)
    compose(0, 0)
    prefix_maps()
    gather(0, 1)
    map_send()
    rest(1, late)

    @pl.when(zhi == 0)
    def _():
        enter(0, 1)

    loads["ar0"].wait()
    maps_rest(0)
    rest(0, early)
    gather(0, 0)
    rest(0, late)

    @pl.when(zhi == 1)
    def _():
        enter(0, 1)

    inflows(0, 1)
    pass_on()
    lag(1)
    enter(0, 0)
    inflows(0, 0)
    lag(0)
    lat_arrival(1)

    chain(1, 0)
    chain(1, 1)
    compose(1, 0)
    compose(1, 1)
    rest(0, range(rows))
    rest(1, range(rows))

    def sent(it):
        for c in range(cols):
            s1_copy(it, c).wait_send()
            s4_copy(it, c).wait_send()
            for d in range(1, YS):
                s2_copy(it, c, d).wait_send()

        @pl.when(zhi == 0)
        def _():
            for c in range(cols):
                for k in range(2):
                    z_copy(it, c, k).wait_send()

        @pl.when(lat < lats - 1)
        def _():
            if it == 0:
                lat_copy(it).wait_send()
            else:
                for k in range(2):
                    part_copy(k).wait_send()

        if it == 1:

            @pl.when(relays)
            def _():
                relay_copy().wait_send()

    t_copy.wait_send()
    for d in range(1, YS):
        tc_copy(d).wait_send()

    @pl.when(lat < lats - 1)
    def _():
        x_copy().wait_send()
        r_copy().wait_send()

    sent(0)
    gather(1, 0)
    gather(1, 1)
    enter(1, 0)
    inflows(1, 0)
    finish(0)
    enter(1, 1)
    inflows(1, 1)
    finish(1)
    sent(1)


def cat_lanes(t, width):
    face = t.shape[0]
    return jnp.concatenate([jnp.zeros((face, width - face), F32), t], axis=1)


def per_device(inverse, upwind, lateral, inlet_trace, previous, uptake_rate, affinity, flow_order):
    operands = (flow_order, inverse, upwind, lateral, inlet_trace, previous, uptake_rate, affinity)
    hbm = pl.BlockSpec(memory_space=pltpu.HBM)
    vmem = pl.BlockSpec(memory_space=pltpu.VMEM)
    dma = pltpu.SemaphoreType.DMA
    scratch = [
        pltpu.SMEM((2, 1, 4), jnp.int32),
        pltpu.VMEM((2, 64, 256), F32),
        pltpu.VMEM((256,), F32),
        pltpu.VMEM((256,), F32),
        pltpu.VMEM((2, 4, 512, 512), BF16),
        pltpu.VMEM((2, 4, 256, 512), BF16),
        pltpu.VMEM((2, 4, 512, 256), BF16),
        pltpu.VMEM((2, 4, 512, 256), BF16),
        pltpu.VMEM((2, 4, 512, 256), BF16),
        pltpu.VMEM((2, 4, 512, 256), F32),
        pltpu.VMEM((2, 2, 4, 512, 256), BF16),
        pltpu.VMEM((2, 4, 64, 256), F32),
        pltpu.VMEM((2, 4, 64, 256), F32),
        pltpu.VMEM((2, 2, 4, 64, 256), BF16),
        pltpu.VMEM((2, 3, 64, 256), F32),
        pltpu.VMEM((2, 2, 4, 64, 64), BF16),
        pltpu.VMEM((2, 2, 4, 64, 256), BF16),
        pltpu.VMEM((2, 64, 64), F32),
        pltpu.VMEM((2, 64, 64), F32),
        pltpu.VMEM((4, 2, 64, 64), F32),
        pltpu.VMEM((2, 2, 2, 64, 64), BF16),
        pltpu.VMEM((2, 2, 192, 320), BF16),
        pltpu.VMEM((2, 2, 2, 64, 128), F32),
        pltpu.VMEM((2, 2, 64, 128), F32),
        pltpu.VMEM((2, 2, 5, 64, 128), F32),
        pltpu.VMEM((2, 2, 64, 128), F32),
        pltpu.VMEM((2, 2, 2, 64, 128), F32),
        pltpu.VMEM((2, 2, 64, 128), F32),
        pltpu.VMEM((2, 2, 2, 64, 128), F32),
        pltpu.VMEM((2, 2, 64, 64), BF16),
        pltpu.VMEM((2, 2, 64, 256), F32),
        pltpu.VMEM((64, 256), F32),
        pltpu.VMEM((2, 64, 128), F32),
        pltpu.VMEM((2, 64, 128), F32),
        pltpu.VMEM((2, 64, 256), F32),
        dma((18,)),
        dma((3,)), dma((3,)),
        dma, dma,
        dma((3,)), dma((4,)),
        dma((2, 2)), dma((2, 2)),
        dma((2, 2, 3)), dma((2, 2, 4)),
        dma((2, 2, 2)), dma((2, 2, 2)),
        dma((2, 2)), dma((2, 2)),
        dma, dma, dma, dma,
        dma, dma,
        pltpu.SemaphoreType.REGULAR,
    ]
    return pl.pallas_call(
        kernel,
        out_shape=jax.ShapeDtypeStruct(previous.shape, BF16),
        in_specs=[hbm] * 8,
        out_specs=vmem,
        scratch_shapes=scratch,
        compiler_params=pltpu.CompilerParams(
            collective_id=0, has_side_effects=True, vmem_limit_bytes=40 * 1024 * 1024
        ),
    )(*(pltpu.with_memory_space_constraint(a, pltpu.HBM) for a in operands))


def solution(mesh):
    placed = (
        P("lat", "stream", None, None, None),
        P("lat", "stream", None, None, None),
        P("lat", "stream", None, None, None),
        P("lat", None, None),
        P("lat", "stream", None, None, None),
        P(),
        P(),
        P("lat", "stream", None),
    )
    return jax.shard_map(
        per_device,
        mesh=mesh,
        in_specs=placed,
        out_specs=P("lat", "stream", None, None, None),
        check_vma=False,
    )
```

```python
import functools

import jax
import jax.numpy as jnp
from jax import lax
from jax.experimental import pallas as pl
from jax.experimental.pallas import tpu as pltpu
from jax.sharding import PartitionSpec as P

MESH = pl.DeviceIdType.MESH
F32 = jnp.float32
BF16 = jnp.bfloat16
YS = 4


def split(x):
    hi = x.astype(BF16)
    return hi, (x - hi.astype(F32)).astype(BF16)


def dot(a, b):
    return jnp.dot(a, b, preferred_element_type=F32)


def dot_nt(a, b):
    return lax.dot_general(a, b, (((1,), (1,)), ((), ())), preferred_element_type=F32)


def dot3(ah, al, b):
    bh, bl = split(b)
    return dot(ah, bh) + (dot(al, bh) + dot(ah, bl))


def cat0(*xs):
    return jnp.concatenate(xs, axis=0)


def kernel(
    order_in, inv, up, side, inlet_in, prev, upt_in, aff_in, out,
    order, inlet, upt, aff, A, UL, PV, MM, NN, F, SRC, LS, LR, LAT, H, G, INF, TT, TP, TC, THL, VV,
    OS, OR, OC, X8S, X8R, YSND, XIN, VO, XE, XL, RS, RR, RL,
    ld_sem, lat_s, lat_r, t_s, t_r, tc_s, tc_r, s1_s, s1_r, s2_s, s2_r, z_s, z_r, s4_s, s4_r, x_s, x_r, r_s, r_r, rl_s, rl_r, ready,
):
    cols, rows, nodes, face = 2, 4, 512, 64
    half = 128
    edge = nodes - face
    s = lax.axis_index("stream")
    lat = lax.axis_index("lat")
    lats = lax.axis_size("lat")
    core = lax.rem(s, 2)
    y = lax.rem(s // 2, YS)
    zhi = s // (2 * YS)
    is0 = core == 0
    xs = 4
    bends = (lax.rem(lat, xs) == xs - 1) & (lat < lats - 1)
    relays = (lax.rem(lat, xs) == xs - 2) & (lat < lats - 2)
    relayed = (lax.rem(lat, xs) == 0) & (lat > 0)
    partner = {"stream": s + 1 - 2 * core}

    def ypeer(d):
        return {"stream": zhi * (2 * YS) + lax.rem(y + d, YS) * 2 + core}


    def above(k):
        return {"stream": 2 * YS + 2 * y + k}

    def below(k):
        return {"stream": 2 * y + k}

    barrier = pltpu.get_barrier_semaphore()

    def hello(peer):
        pl.semaphore_signal(barrier, inc=1, device_id=peer, device_id_type=MESH)

    for peer in (partner, ypeer(1), ypeer(2), ypeer(3)):
        hello(peer)

    @pl.when(lat > 0)
    def _():
        hello({"lat": lat - 1})

    @pl.when(relays)
    def _():
        hello({"lat": lat + 1})

    @pl.when(relayed)
    def _():
        hello({"lat": lat - 2})

    @pl.when(zhi == 0)
    def _():
        hello(above(0))
        hello(above(1))

    expected = 4 + jnp.where(lat < lats - 1, 1, 0) + jnp.where(zhi == 1, 2, 0)
    expected = expected + jnp.where(bends, 1, 0) + jnp.where(relays, 1, 0)

    loads = {}

    def load(name, k, src, dst):
        c = pltpu.make_async_copy(src, dst, ld_sem.at[k])
        c.start()
        loads[name] = c

    load("prev1", 0, prev.at[1, 0], PV.at[1])
    for c in (1, 0):
        for k in range(2):
            load(f"u{c}{k}", 2 + 2 * c + k, up.at[c, 0], UL.at[c, :, k * face : (k + 1) * face])
            load(f"l{c}{k}", 6 + 2 * c + k, side.at[c, 0], UL.at[c, :, (2 + k) * face : (3 + k) * face])
        load(f"al{c}", 10 + c, inv.at[c, 0, :, edge:], A.at[c, :, edge:])
        if c:
            load("order", 14, order_in, order)
            load("upt", 15, upt_in, upt)
            load("aff", 16, aff_in, aff)
    load("prev0", 1, prev.at[0, 0], PV.at[0])
    load("inlet", 17, inlet_in, inlet)
    load("ar1", 13, inv.at[1, 0, :, 0:edge], A.at[1, :, 0:edge])
    load("ar0", 12, inv.at[0, 0, :, 0:edge], A.at[0, :, 0:edge])

    def remote(src, dst, ssem, rsem, peer):
        return pltpu.make_async_remote_copy(
            src_ref=src, dst_ref=dst, send_sem=ssem, recv_sem=rsem, device_id=peer, device_id_type=MESH
        )

    def lat_copy(it):
        return remote(LS.at[it], LR.at[it], lat_s.at[it], lat_r.at[it], {"lat": lax.rem(lat + 1, lats)})

    def lat_send(it):
        @pl.when(lat < lats - 1)
        def _():
            lat_copy(it).start()

    def prev_trace(c, j):
        parts = []
        for a in range(8):
            piece = PV[c, j, a * 64 + 48 : a * 64 + 64, :].astype(F32)
            parts.append(piece[8:16])
        return cat0(*parts)

    def value_trace(x):
        return cat0(*[x[a * 64 + 56 : a * 64 + 64] for a in range(8)])

    def apply(m4, h, l):
        return dot(m4, cat0(h, l, h, l))

    def put_maps(c, j, rows_of):
        hi, lo = split(dot_nt(A[c, j, rows_of, :], UL[c, j]))
        MM[c, j, rows_of, 0:128] = hi[:, 0:128]
        MM[c, j, rows_of, 128:256] = lo[:, 0:128]
        NN[c, j, rows_of, 0:128] = hi[:, 128:256]
        NN[c, j, rows_of, 128:256] = lo[:, 128:256]

    def edge_maps(c):
        for n in (f"u{c}0", f"u{c}1", f"l{c}0", f"l{c}1", f"al{c}"):
            loads[n].wait()
        for j in range(rows):
            put_maps(c, j, slice(edge, nodes))

    loads["prev1"].wait()
    for j in range(rows):
        LS[0, j] = prev_trace(1, j)
    pl.semaphore_wait(barrier, expected)
    lat_send(0)

    @pl.when(zhi == 1)
    def _():
        for k in range(2):
            pl.semaphore_signal(ready, inc=1, device_id=below(k), device_id_type=MESH)

    edge_maps(1)

    edge_maps(0)
    loads["order"].wait()

    def mm_edge(c, j):
        return MM[c, j, edge:, :]

    eye_row = lax.broadcasted_iota(jnp.int32, (face, face), 0)
    eye_lane = lax.broadcasted_iota(jnp.int32, (face, face), 1)
    eye = jnp.where(eye_row == eye_lane, 1.0, 0.0).astype(BF16)
    for c in range(cols):
        G[c, 0, 0] = eye
        G[c, 1, 0] = jnp.zeros((face, face), BF16)
        first = mm_edge(c, order[c, 0, 0])
        g = first[:, 0:face].astype(F32) + first[:, 128 : 128 + face].astype(F32)
        for p in range(1, rows + 1):
            if p < rows:
                gh, gl = split(g)
                G[c, 0, p] = gh
                G[c, 1, p] = gl
                g = apply(mm_edge(c, order[c, 0, p]), gh, gl)
        TT[c] = g
    t_copy = remote(TT, TP, t_s, t_r, partner)
    t_copy.start()

    loads["prev0"].wait()
    for j in range(rows):
        LAT[0, 1, j] = prev_trace(0, j).astype(BF16)
        LAT[1, 1, j] = jnp.zeros((face, 256), BF16)
    loads["inlet"].wait()
    loads["upt"].wait()
    loads["aff"].wait()
    for c in range(cols):
        piece = jnp.where(is0, inlet[c, :, 0:half], inlet[c, :, half:])
        piece = jnp.where(zhi == 0, piece, jnp.zeros_like(piece))
        for it in range(2):
            OC[it, c, YS] = piece

    rate = upt[...].reshape(1, 256)
    affinity = aff[...].reshape(1, 256)

    inv_rate = 1.0 / rate
    ratio = affinity * inv_rate

    def source_of(x):
        return x / (inv_rate + ratio * jnp.abs(x))

    def put_source(c, j, x):
        hi, lo = split(source_of(x))
        SRC[c, 0, j] = hi
        SRC[c, 1, j] = lo
        a = A[c, j, edge:, :]
        F[c, j, edge:, :] = dot(a, hi) + dot(a, lo)

    def first_source(c):
        for j in range(rows):
            put_source(c, j, PV[c, j].astype(F32))

    def rest(c, js):
        for j in js:
            a = A[c, j, 0:edge, :]
            side_part = apply(NN[c, j, 0:edge, :], LAT[0, c, j], LAT[1, c, j])
            F[c, j, 0:edge, :] = dot(a, SRC[c, 0, j]) + dot(a, SRC[c, 1, j]) + side_part

    def maps_rest(c):
        for j in range(rows):
            put_maps(c, j, slice(0, edge))

    zero_trace = jnp.zeros((face, 256), BF16)

    def s1_copy(it, c):
        return remote(OS.at[it, c, 1 - core], OR.at[it, c], s1_s.at[it, c], s1_r.at[it, c], partner)

    def chain(it, *cs):
        for c in cs:
            for j in range(rows):
                F[c, j, edge:, :] += apply(NN[c, j, edge:, :], LAT[0, c, j], LAT[1, c, j])
        hs = [F[c, order[c, 0, 0], edge:, :] for c in cs]
        for p in range(1, rows):
            for i, c in enumerate(cs):
                H[c, p - 1] = hs[i]
                hh, hl = split(hs[i])
                j = order[c, 0, p]
                hs[i] = F[c, j, edge:, :] + apply(mm_edge(c, j), hh, hl)
        for i, c in enumerate(cs):
            OS[it, c, 0] = hs[i][:, 0:half]
            OS[it, c, 1] = hs[i][:, half:]
        for c in cs:
            s1_copy(it, c).start()

    def first_second(it, c):
        own, got = OS[it, c, core], OR[it, c]
        return jnp.where(is0, own, got), jnp.where(is0, got, own)

    def s2_copy(it, c, d):
        return remote(OC.at[it, c, y], OC.at[it, c, y], s2_s.at[it, c, d - 1], s2_r.at[it, c, y], ypeer(d))

    def s2_arrival(it, c, d):
        source = lax.rem(y + d, YS)
        return remote(OC.at[it, c, source], OC.at[it, c, source], s2_s.at[it, c, d - 1], s2_r.at[it, c, source], ypeer(d))

    def compose(it, c):
        s1_copy(it, c).wait_recv()
        o_first, o_second = first_second(it, c)
        OC[it, c, y] = dot3(THL[1, c, 0], THL[1, c, 1], o_first) + o_second
        for d in (2, 1, 3):
            s2_copy(it, c, d).start()

    def z_copy(it, c, k):
        return remote(X8S.at[it, c], X8R.at[it, c, core], z_s.at[it, c, k], z_r.at[it, c, core], above(k))

    def z_arrival(it, c, h):
        return remote(X8S.at[it, c], X8R.at[it, c, h], z_s.at[it, c, h], z_r.at[it, c, h], partner)

    def s4_copy(it, c):
        return remote(YSND.at[it, c], XIN.at[it, c, core], s4_s.at[it, c], s4_r.at[it, c], partner)

    def s4_arrival(it, c):
        return remote(YSND.at[it, c], XIN.at[it, c, 1 - core], s4_s.at[it, c], s4_r.at[it, c], partner)

    def gather(it, c):
        for d in (1, 3, 2):
            s2_arrival(it, c, d).wait_recv()
        offsets = OC[it, c].reshape((YS + 1) * face, half)
        q = dot3(VV[c, 0], VV[c, 1], offsets)
        o_first, _ = first_second(it, c)
        first, second = q[0:face], q[face : 2 * face] + o_first

        @pl.when(zhi == 0)
        def _():
            X8S[it, c] = q[2 * face :]
            if it == 0 and c == 1:
                pl.semaphore_wait(ready, 2)
            for k in range(2):
                z_copy(it, c, k).start()

        YSND[it, c] = jnp.where(is0, second, first)
        XIN[it, c, core] = jnp.where(is0, first, second)
        s4_copy(it, c).start()

    def x_copy():
        return remote(XE.at[0, 1], XL, x_s, x_r, {"lat": lax.rem(lat + 1, lats)})

    def r_copy():
        return remote(RS, RR, r_s, r_r, {"lat": lax.rem(lat + 1, lats)})

    def enter(it, c):
        s4_arrival(it, c).wait_recv()
        XE[it, c] = jnp.concatenate([XIN[it, c, 0], XIN[it, c, 1]], axis=1)

        @pl.when(zhi == 1)
        def _():
            for h in range(2):
                z_arrival(it, c, h).wait_recv()
            carried = jnp.concatenate([X8R[it, c, 0], X8R[it, c, 1]], axis=1)
            XE[it, c] += dot3(VO[c, 0], VO[c, 1], carried)

        if it == 0 and c == 1:

            @pl.when(lat < lats - 1)
            def _():
                x_copy().start()

    def inflows(it, c):
        xh, xl = split(XE[it, c])
        INF[0, c, 0] = xh
        INF[1, c, 0] = xl
        gh = G[c, 0, 1:].reshape((rows - 1) * face, face)
        gl = G[c, 1, 1:].reshape((rows - 1) * face, face)
        later = dot(gh, xh) + (dot(gl, xh) + dot(gh, xl))
        for p in range(1, rows):
            xh, xl = split(later[(p - 1) * face : p * face] + H[c, p - 1])
            INF[0, c, p] = xh
            INF[1, c, p] = xl

    def rank_of(c, j):
        rank = jnp.int32(0)
        for p in range(1, rows):
            rank = jnp.where(order[c, 0, p] == j, p, rank)
        return rank

    def solved(c, j):
        rank = rank_of(c, j)
        return F[c, j] + apply(MM[c, j], INF[0, c, rank], INF[1, c, rank])

    def traces_ahead():
        maps = []
        for j in range(rows):
            a = cat0(*[A[1, j, i * 64 + 48 : i * 64 + 64, :].astype(F32)[8:16] for i in range(8)]).astype(BF16)
            hi, lo = split(dot_nt(a, UL[1, j]))
            mt = jnp.concatenate([hi[:, 0:128], lo[:, 0:128]], axis=1)
            nt = jnp.concatenate([hi[:, 128:256], lo[:, 128:256]], axis=1)
            rank = rank_of(1, j)
            hh, hl = split(jnp.where(rank > 0, H[1, jnp.maximum(rank - 1, 0)], 0.0))
            base = dot(a, SRC[1, 0, j]) + dot(a, SRC[1, 1, j])
            LS[1, j] = base + apply(nt, LAT[0, 1, j], LAT[1, 1, j]) + apply(mt, hh, hl)
            maps.append(apply(mt, G[1, 0, rank], G[1, 1, rank]))
        for k in range(2):
            RS[k] = jnp.concatenate([maps[2 * k], maps[2 * k + 1]], axis=1)


        @pl.when(lat < lats - 1)
        def _():
            part_copy(0).start()

        @pl.when((lat < lats - 1) & jnp.logical_not(bends))
        def _():
            part_copy(1).start()
            r_copy().start()

        @pl.when(bends)
        def _():
            bend_copy().start()

    def map_send():
        @pl.when(bends)
        def _():
            r_copy().start()

    def part_copy(k):
        js = pl.ds(2 * k, 2)
        return remote(LS.at[1, js], LR.at[1, js], lat_s.at[1 + k], lat_r.at[1 + k], {"lat": lax.rem(lat + 1, lats)})

    back = pl.ds(2, 2)

    def bend_copy():
        peer = {"lat": lax.rem(lat + lats - 1, lats)}
        return remote(LS.at[1, back], RL, lat_s.at[2], rl_r, peer)

    def relay_copy():
        peer = {"lat": lax.rem(lat + 2, lats)}
        return remote(RL, LR.at[1, back], rl_s, lat_r.at[2], peer)

    def pass_on():
        @pl.when(relays)
        def _():
            bend_copy().wait_recv()
            relay_copy().start()

    def lag(c):
        for j in range(rows):
            x = solved(c, j)
            if c == 0:
                hi, lo = split(value_trace(x))
                LAT[0, 1, j] = hi
                LAT[1, 1, j] = lo
            put_source(c, j, x)

    def finish(c):
        for j in range(rows):
            out[c, 0, j] = solved(c, j).astype(BF16)

    def lat_arrival(it):
        @pl.when(lat > 0)
        def _():
            if it == 0:
                lat_copy(it).wait_recv()
            else:
                for k in range(2):
                    part_copy(k).wait_recv()
                r_copy().wait_recv()
                x_copy().wait_recv()
                xh, xl = split(XL[...])
            for j in range(rows):
                trace = LR[it, j]
                if it == 1:
                    rh, rl = split(RR[j // 2][:, (j % 2) * face : (j % 2 + 1) * face])
                    trace = trace + (dot(rh, xh) + (dot(rl, xh) + dot(rh, xl)))
                hi, lo = split(trace)
                LAT[0, 0, j] = hi
                LAT[1, 0, j] = lo

        @pl.when(lat == 0)
        def _():
            for j in range(rows):
                LAT[0, 0, j] = zero_trace
                LAT[1, 0, j] = zero_trace

    def prefix_maps():
        for d in (1, 3, 2):
            tc_arrival(d).wait_recv()
        width = (YS + 1) * face
        row_id = lax.broadcasted_iota(jnp.int32, (face, width), 0)
        lane_id = lax.broadcasted_iota(jnp.int32, (face, width), 1)

        def unit(block):
            return jnp.where(lane_id - face * block == row_id, 1.0, 0.0).astype(F32)

        for c in range(cols):
            x = unit(YS)
            mine = jnp.where(y == 0, x, jnp.zeros_like(x))
            for t in range(YS):
                if t == 0:
                    x = cat_lanes(TC[0, c], width) + unit(0)
                else:
                    th, tl = split(TC[t, c])
                    x = dot3(th, tl, x) + unit(t)
                if t + 1 < YS:
                    mine = jnp.where(y == t + 1, x, mine)
            both = dot3(THL[0, c, 0], THL[0, c, 1], mine)
            vh, vl = split(cat0(mine, both, x))
            VV[c, 0] = vh
            VV[c, 1] = vl
            v = slice(YS * face, (YS + 1) * face)
            VO[c, 0] = jnp.where(is0, vh[0:face, v], vh[face : 2 * face, v])
            VO[c, 1] = jnp.where(is0, vl[0:face, v], vl[face : 2 * face, v])

    first_source(1)

    t_copy.wait_recv()
    for c in range(cols):
        own, got = TT[c], TP[c]
        t0h, t0l = split(jnp.where(is0, own, got))
        t1h, t1l = split(jnp.where(is0, got, own))
        THL[0, c, 0], THL[0, c, 1], THL[1, c, 0], THL[1, c, 1] = t0h, t0l, t1h, t1l
        TC[y, c] = dot3(t1h, t1l, jnp.where(is0, own, got))

    def tc_copy(d):
        return remote(TC.at[y], TC.at[y], tc_s.at[d - 1], tc_r.at[y], ypeer(d))

    def tc_arrival(d):
        source = lax.rem(y + d, YS)
        return remote(TC.at[source], TC.at[source], tc_s.at[d - 1], tc_r.at[source], ypeer(d))

    for d in (2, 1, 3):
        tc_copy(d).start()

    chain(0, 1)
    first_source(0)
    compose(0, 1)
    loads["ar1"].wait()
    traces_ahead()
    maps_rest(1)

    early, late = range(0, 2), range(2, rows)
    lat_arrival(0)
    chain(0, 0)
    rest(1, early)
    compose(0, 0)
    prefix_maps()
    gather(0, 1)
    map_send()
    rest(1, late)

    @pl.when(zhi == 0)
    def _():
        enter(0, 1)

    pass_on()
    loads["ar0"].wait()
    maps_rest(0)
    rest(0, early)
    gather(0, 0)
    rest(0, late)

    @pl.when(zhi == 1)
    def _():
        enter(0, 1)

    inflows(0, 1)
    lag(1)
    enter(0, 0)
    inflows(0, 0)
    lag(0)
    lat_arrival(1)

    chain(1, 0, 1)
    compose(1, 0)
    compose(1, 1)
    rest(0, range(rows))
    rest(1, range(rows))

    def sent(it):
        for c in range(cols):
            s1_copy(it, c).wait_send()
            s4_copy(it, c).wait_send()
            for d in range(1, YS):
                s2_copy(it, c, d).wait_send()

        @pl.when(zhi == 0)
        def _():
            for c in range(cols):
                for k in range(2):
                    z_copy(it, c, k).wait_send()

        @pl.when(lat < lats - 1)
        def _():
            if it == 0:
                lat_copy(it).wait_send()
            else:
                for k in range(2):
                    part_copy(k).wait_send()

        if it == 1:

            @pl.when(relays)
            def _():
                relay_copy().wait_send()

    t_copy.wait_send()
    for d in range(1, YS):
        tc_copy(d).wait_send()

    @pl.when(lat < lats - 1)
    def _():
        x_copy().wait_send()
        r_copy().wait_send()

    sent(0)
    gather(1, 0)
    gather(1, 1)
    enter(1, 0)
    inflows(1, 0)
    finish(0)
    enter(1, 1)
    inflows(1, 1)
    finish(1)
    sent(1)


def cat_lanes(t, width):
    face = t.shape[0]
    return jnp.concatenate([jnp.zeros((face, width - face), F32), t], axis=1)


def per_device(inverse, upwind, lateral, inlet_trace, previous, uptake_rate, affinity, flow_order):
    operands = (flow_order, inverse, upwind, lateral, inlet_trace, previous, uptake_rate, affinity)
    hbm = pl.BlockSpec(memory_space=pltpu.HBM)
    vmem = pl.BlockSpec(memory_space=pltpu.VMEM)
    dma = pltpu.SemaphoreType.DMA
    scratch = [
        pltpu.SMEM((2, 1, 4), jnp.int32),
        pltpu.VMEM((2, 64, 256), F32),
        pltpu.VMEM((256,), F32),
        pltpu.VMEM((256,), F32),
        pltpu.VMEM((2, 4, 512, 512), BF16),
        pltpu.VMEM((2, 4, 256, 512), BF16),
        pltpu.VMEM((2, 4, 512, 256), BF16),
        pltpu.VMEM((2, 4, 512, 256), BF16),
        pltpu.VMEM((2, 4, 512, 256), BF16),
        pltpu.VMEM((2, 4, 512, 256), F32),
        pltpu.VMEM((2, 2, 4, 512, 256), BF16),
        pltpu.VMEM((2, 4, 64, 256), F32),
        pltpu.VMEM((2, 4, 64, 256), F32),
        pltpu.VMEM((2, 2, 4, 64, 256), BF16),
        pltpu.VMEM((2, 3, 64, 256), F32),
        pltpu.VMEM((2, 2, 4, 64, 64), BF16),
        pltpu.VMEM((2, 2, 4, 64, 256), BF16),
        pltpu.VMEM((2, 64, 64), F32),
        pltpu.VMEM((2, 64, 64), F32),
        pltpu.VMEM((4, 2, 64, 64), F32),
        pltpu.VMEM((2, 2, 2, 64, 64), BF16),
        pltpu.VMEM((2, 2, 192, 320), BF16),
        pltpu.VMEM((2, 2, 2, 64, 128), F32),
        pltpu.VMEM((2, 2, 64, 128), F32),
        pltpu.VMEM((2, 2, 5, 64, 128), F32),
        pltpu.VMEM((2, 2, 64, 128), F32),
        pltpu.VMEM((2, 2, 2, 64, 128), F32),
        pltpu.VMEM((2, 2, 64, 128), F32),
        pltpu.VMEM((2, 2, 2, 64, 128), F32),
        pltpu.VMEM((2, 2, 64, 64), BF16),
        pltpu.VMEM((2, 2, 64, 256), F32),
        pltpu.VMEM((64, 256), F32),
        pltpu.VMEM((2, 64, 128), F32),
        pltpu.VMEM((2, 64, 128), F32),
        pltpu.VMEM((2, 64, 256), F32),
        dma((18,)),
        dma((3,)), dma((3,)),
        dma, dma,
        dma((3,)), dma((4,)),
        dma((2, 2)), dma((2, 2)),
        dma((2, 2, 3)), dma((2, 2, 4)),
        dma((2, 2, 2)), dma((2, 2, 2)),
        dma((2, 2)), dma((2, 2)),
        dma, dma, dma, dma,
        dma, dma,
        pltpu.SemaphoreType.REGULAR,
    ]
    return pl.pallas_call(
        kernel,
        out_shape=jax.ShapeDtypeStruct(previous.shape, BF16),
        in_specs=[hbm] * 8,
        out_specs=vmem,
        scratch_shapes=scratch,
        compiler_params=pltpu.CompilerParams(
            collective_id=0, has_side_effects=True, vmem_limit_bytes=40 * 1024 * 1024
        ),
    )(*(pltpu.with_memory_space_constraint(a, pltpu.HBM) for a in operands))


def solution(mesh):
    placed = (
        P("lat", "stream", None, None, None),
        P("lat", "stream", None, None, None),
        P("lat", "stream", None, None, None),
        P("lat", None, None),
        P("lat", "stream", None, None, None),
        P(),
        P(),
        P("lat", "stream", None),
    )
    return jax.shard_map(
        per_device,
        mesh=mesh,
        in_specs=placed,
        out_specs=P("lat", "stream", None, None, None),
        check_vma=False,
    )
```

```python
import functools

import jax
import jax.numpy as jnp
from jax import lax
from jax.experimental import pallas as pl
from jax.experimental.pallas import tpu as pltpu
from jax.sharding import PartitionSpec as P

MESH = pl.DeviceIdType.MESH
F32 = jnp.float32
BF16 = jnp.bfloat16
YS = 4


def split(x):
    hi = x.astype(BF16)
    return hi, (x - hi.astype(F32)).astype(BF16)


def dot(a, b):
    return jnp.dot(a, b, preferred_element_type=F32)


def dot_nt(a, b):
    return lax.dot_general(a, b, (((1,), (1,)), ((), ())), preferred_element_type=F32)


def dot3(ah, al, b):
    bh, bl = split(b)
    return dot(ah, bh) + (dot(al, bh) + dot(ah, bl))


def cat0(*xs):
    return jnp.concatenate(xs, axis=0)


def kernel(
    order_in, inv, up, side, inlet_in, prev, upt_in, aff_in, out,
    order, inlet, upt, aff, A, UL, PV, MM, NN, F, SRC, LS, LR, LAT, H, G, INF, TT, TP, TC, THL, VV,
    OS, OR, OC, X8S, X8R, YSND, XIN, VO, XE, XL, RS, RR, RL,
    ld_sem, lat_s, lat_r, t_s, t_r, tc_s, tc_r, s1_s, s1_r, s2_s, s2_r, z_s, z_r, s4_s, s4_r, x_s, x_r, r_s, r_r, rl_s, rl_r, ready,
):
    cols, rows, nodes, face = 2, 4, 512, 64
    half = 128
    edge = nodes - face
    s = lax.axis_index("stream")
    lat = lax.axis_index("lat")
    lats = lax.axis_size("lat")
    core = lax.rem(s, 2)
    y = lax.rem(s // 2, YS)
    zhi = s // (2 * YS)
    is0 = core == 0
    xs = 4
    bends = (lax.rem(lat, xs) == xs - 1) & (lat < lats - 1)
    relays = (lax.rem(lat, xs) == xs - 2) & (lat < lats - 2)
    relayed = (lax.rem(lat, xs) == 0) & (lat > 0)
    starts = (lax.rem(lat, xs) == 0) & (lat < lats - xs)
    partner = {"stream": s + 1 - 2 * core}

    def ypeer(d):
        return {"stream": zhi * (2 * YS) + lax.rem(y + d, YS) * 2 + core}


    def above(k):
        return {"stream": 2 * YS + 2 * y + k}

    def below(k):
        return {"stream": 2 * y + k}

    barrier = pltpu.get_barrier_semaphore()

    def hello(peer):
        pl.semaphore_signal(barrier, inc=1, device_id=peer, device_id_type=MESH)

    for peer in (partner, ypeer(1), ypeer(2), ypeer(3)):
        hello(peer)

    @pl.when(lat > 0)
    def _():
        hello({"lat": lat - 1})

    @pl.when(relays)
    def _():
        hello({"lat": lat + 1})

    @pl.when(starts)
    def _():
        hello({"lat": lat + xs - 1})

    @pl.when(relayed)
    def _():
        hello({"lat": lat - 2})
        hello({"lat": lat - xs})

    @pl.when(zhi == 0)
    def _():
        hello(above(0))
        hello(above(1))

    expected = 4 + jnp.where(lat < lats - 1, 1, 0) + jnp.where(zhi == 1, 2, 0)
    expected = expected + jnp.where(bends, 2, 0) + jnp.where(relays | starts, 1, 0)

    loads = {}

    def load(name, k, src, dst):
        c = pltpu.make_async_copy(src, dst, ld_sem.at[k])
        c.start()
        loads[name] = c

    load("prev1", 0, prev.at[1, 0], PV.at[1])
    for c in (1, 0):
        for k in range(2):
            load(f"u{c}{k}", 2 + 2 * c + k, up.at[c, 0], UL.at[c, :, k * face : (k + 1) * face])
            load(f"l{c}{k}", 6 + 2 * c + k, side.at[c, 0], UL.at[c, :, (2 + k) * face : (3 + k) * face])
        load(f"al{c}", 10 + c, inv.at[c, 0, :, edge:], A.at[c, :, edge:])
        if c:
            load("order", 14, order_in, order)
            load("upt", 15, upt_in, upt)
            load("aff", 16, aff_in, aff)
    load("prev0", 1, prev.at[0, 0], PV.at[0])
    load("inlet", 17, inlet_in, inlet)
    load("ar1", 13, inv.at[1, 0, :, 0:edge], A.at[1, :, 0:edge])
    load("ar0", 12, inv.at[0, 0, :, 0:edge], A.at[0, :, 0:edge])

    def remote(src, dst, ssem, rsem, peer):
        return pltpu.make_async_remote_copy(
            src_ref=src, dst_ref=dst, send_sem=ssem, recv_sem=rsem, device_id=peer, device_id_type=MESH
        )

    def lat_copy(it):
        return remote(LS.at[it], LR.at[it], lat_s.at[it], lat_r.at[it], {"lat": lax.rem(lat + 1, lats)})

    def lat_send(it):
        @pl.when(lat < lats - 1)
        def _():
            lat_copy(it).start()

    def prev_trace(c, j):
        parts = []
        for a in range(8):
            piece = PV[c, j, a * 64 + 48 : a * 64 + 64, :].astype(F32)
            parts.append(piece[8:16])
        return cat0(*parts)

    def value_trace(x):
        return cat0(*[x[a * 64 + 56 : a * 64 + 64] for a in range(8)])

    def apply(m4, h, l):
        return dot(m4, cat0(h, l, h, l))

    def put_maps(c, j, rows_of):
        hi, lo = split(dot_nt(A[c, j, rows_of, :], UL[c, j]))
        MM[c, j, rows_of, 0:128] = hi[:, 0:128]
        MM[c, j, rows_of, 128:256] = lo[:, 0:128]
        NN[c, j, rows_of, 0:128] = hi[:, 128:256]
        NN[c, j, rows_of, 128:256] = lo[:, 128:256]

    def edge_maps(c):
        for n in (f"u{c}0", f"u{c}1", f"l{c}0", f"l{c}1", f"al{c}"):
            loads[n].wait()
        for j in range(rows):
            put_maps(c, j, slice(edge, nodes))

    loads["prev1"].wait()
    for j in range(rows):
        LS[0, j] = prev_trace(1, j)
    pl.semaphore_wait(barrier, expected)
    lat_send(0)

    @pl.when(zhi == 1)
    def _():
        for k in range(2):
            pl.semaphore_signal(ready, inc=1, device_id=below(k), device_id_type=MESH)

    edge_maps(1)

    edge_maps(0)
    loads["order"].wait()

    def mm_edge(c, j):
        return MM[c, j, edge:, :]

    eye_row = lax.broadcasted_iota(jnp.int32, (face, face), 0)
    eye_lane = lax.broadcasted_iota(jnp.int32, (face, face), 1)
    eye = jnp.where(eye_row == eye_lane, 1.0, 0.0).astype(BF16)
    for c in range(cols):
        G[c, 0, 0] = eye
        G[c, 1, 0] = jnp.zeros((face, face), BF16)
        first = mm_edge(c, order[c, 0, 0])
        g = first[:, 0:face].astype(F32) + first[:, 128 : 128 + face].astype(F32)
        for p in range(1, rows + 1):
            if p < rows:
                gh, gl = split(g)
                G[c, 0, p] = gh
                G[c, 1, p] = gl
                g = apply(mm_edge(c, order[c, 0, p]), gh, gl)
        TT[c] = g
    t_copy = remote(TT, TP, t_s, t_r, partner)
    t_copy.start()

    loads["prev0"].wait()
    for j in range(rows):
        LAT[0, 1, j] = prev_trace(0, j).astype(BF16)
        LAT[1, 1, j] = jnp.zeros((face, 256), BF16)
    loads["inlet"].wait()
    loads["upt"].wait()
    loads["aff"].wait()
    for c in range(cols):
        piece = jnp.where(is0, inlet[c, :, 0:half], inlet[c, :, half:])
        piece = jnp.where(zhi == 0, piece, jnp.zeros_like(piece))
        for it in range(2):
            OC[it, c, YS] = piece

    rate = upt[...].reshape(1, 256)
    affinity = aff[...].reshape(1, 256)

    inv_rate = 1.0 / rate
    ratio = affinity * inv_rate

    def source_of(x):
        return x / (inv_rate + ratio * jnp.abs(x))

    def put_source(c, j, x):
        hi, lo = split(source_of(x))
        SRC[c, 0, j] = hi
        SRC[c, 1, j] = lo
        a = A[c, j, edge:, :]
        F[c, j, edge:, :] = dot(a, hi) + dot(a, lo)

    def first_source(c):
        for j in range(rows):
            put_source(c, j, PV[c, j].astype(F32))

    def rest(c, js):
        for j in js:
            a = A[c, j, 0:edge, :]
            side_part = apply(NN[c, j, 0:edge, :], LAT[0, c, j], LAT[1, c, j])
            F[c, j, 0:edge, :] = dot(a, SRC[c, 0, j]) + dot(a, SRC[c, 1, j]) + side_part

    def maps_rest(c):
        for j in range(rows):
            put_maps(c, j, slice(0, edge))

    zero_trace = jnp.zeros((face, 256), BF16)

    def s1_copy(it, c):
        return remote(OS.at[it, c, 1 - core], OR.at[it, c], s1_s.at[it, c], s1_r.at[it, c], partner)

    def chain(it, *cs):
        for c in cs:
            for j in range(rows):
                F[c, j, edge:, :] += apply(NN[c, j, edge:, :], LAT[0, c, j], LAT[1, c, j])
        hs = [F[c, order[c, 0, 0], edge:, :] for c in cs]
        for p in range(1, rows):
            for i, c in enumerate(cs):
                H[c, p - 1] = hs[i]
                hh, hl = split(hs[i])
                j = order[c, 0, p]
                hs[i] = F[c, j, edge:, :] + apply(mm_edge(c, j), hh, hl)
        for i, c in enumerate(cs):
            OS[it, c, 0] = hs[i][:, 0:half]
            OS[it, c, 1] = hs[i][:, half:]
        for c in cs:
            s1_copy(it, c).start()

    def first_second(it, c):
        own, got = OS[it, c, core], OR[it, c]
        return jnp.where(is0, own, got), jnp.where(is0, got, own)

    def s2_copy(it, c, d):
        return remote(OC.at[it, c, y], OC.at[it, c, y], s2_s.at[it, c, d - 1], s2_r.at[it, c, y], ypeer(d))

    def s2_arrival(it, c, d):
        source = lax.rem(y + d, YS)
        return remote(OC.at[it, c, source], OC.at[it, c, source], s2_s.at[it, c, d - 1], s2_r.at[it, c, source], ypeer(d))

    def compose(it, c):
        s1_copy(it, c).wait_recv()
        o_first, o_second = first_second(it, c)
        OC[it, c, y] = dot3(THL[1, c, 0], THL[1, c, 1], o_first) + o_second
        for d in (2, 1, 3):
            s2_copy(it, c, d).start()

    def z_copy(it, c, k):
        return remote(X8S.at[it, c], X8R.at[it, c, core], z_s.at[it, c, k], z_r.at[it, c, core], above(k))

    def z_arrival(it, c, h):
        return remote(X8S.at[it, c], X8R.at[it, c, h], z_s.at[it, c, h], z_r.at[it, c, h], partner)

    def s4_copy(it, c):
        return remote(YSND.at[it, c], XIN.at[it, c, core], s4_s.at[it, c], s4_r.at[it, c], partner)

    def s4_arrival(it, c):
        return remote(YSND.at[it, c], XIN.at[it, c, 1 - core], s4_s.at[it, c], s4_r.at[it, c], partner)

    def gather(it, c):
        for d in (1, 3, 2):
            s2_arrival(it, c, d).wait_recv()
        offsets = OC[it, c].reshape((YS + 1) * face, half)
        q = dot3(VV[c, 0], VV[c, 1], offsets)
        o_first, _ = first_second(it, c)
        first, second = q[0:face], q[face : 2 * face] + o_first

        @pl.when(zhi == 0)
        def _():
            X8S[it, c] = q[2 * face :]
            if it == 0 and c == 1:
                pl.semaphore_wait(ready, 2)
            for k in range(2):
                z_copy(it, c, k).start()

        YSND[it, c] = jnp.where(is0, second, first)
        XIN[it, c, core] = jnp.where(is0, first, second)
        s4_copy(it, c).start()

    def x_copy():
        return remote(XE.at[0, 1], XL, x_s, x_r, {"lat": lax.rem(lat + 1, lats)})

    def r_copy():
        return remote(RS, RR, r_s, r_r, {"lat": lax.rem(lat + 1, lats)})

    def enter(it, c):
        s4_arrival(it, c).wait_recv()
        XE[it, c] = jnp.concatenate([XIN[it, c, 0], XIN[it, c, 1]], axis=1)

        @pl.when(zhi == 1)
        def _():
            for h in range(2):
                z_arrival(it, c, h).wait_recv()
            carried = jnp.concatenate([X8R[it, c, 0], X8R[it, c, 1]], axis=1)
            XE[it, c] += dot3(VO[c, 0], VO[c, 1], carried)

        if it == 0 and c == 1:

            @pl.when(lat < lats - 1)
            def _():
                x_copy().start()

    def inflows(it, c):
        xh, xl = split(XE[it, c])
        INF[0, c, 0] = xh
        INF[1, c, 0] = xl
        gh = G[c, 0, 1:].reshape((rows - 1) * face, face)
        gl = G[c, 1, 1:].reshape((rows - 1) * face, face)
        later = dot(gh, xh) + (dot(gl, xh) + dot(gh, xl))
        for p in range(1, rows):
            xh, xl = split(later[(p - 1) * face : p * face] + H[c, p - 1])
            INF[0, c, p] = xh
            INF[1, c, p] = xl

    def rank_of(c, j):
        rank = jnp.int32(0)
        for p in range(1, rows):
            rank = jnp.where(order[c, 0, p] == j, p, rank)
        return rank

    def solved(c, j):
        rank = rank_of(c, j)
        return F[c, j] + apply(MM[c, j], INF[0, c, rank], INF[1, c, rank])

    def traces_ahead():
        maps = []
        for j in range(rows):
            a = cat0(*[A[1, j, i * 64 + 48 : i * 64 + 64, :].astype(F32)[8:16] for i in range(8)]).astype(BF16)
            hi, lo = split(dot_nt(a, UL[1, j]))
            mt = jnp.concatenate([hi[:, 0:128], lo[:, 0:128]], axis=1)
            nt = jnp.concatenate([hi[:, 128:256], lo[:, 128:256]], axis=1)
            rank = rank_of(1, j)
            hh, hl = split(jnp.where(rank > 0, H[1, jnp.maximum(rank - 1, 0)], 0.0))
            base = dot(a, SRC[1, 0, j]) + dot(a, SRC[1, 1, j])
            LS[1, j] = base + apply(nt, LAT[0, 1, j], LAT[1, 1, j]) + apply(mt, hh, hl)
            maps.append(apply(mt, G[1, 0, rank], G[1, 1, rank]))
        for k in range(2):
            RS[k] = jnp.concatenate([maps[2 * k], maps[2 * k + 1]], axis=1)


        @pl.when(lat < lats - 1)
        def _():
            part_copy(0).start()

        @pl.when((lat < lats - 1) & jnp.logical_not(bends))
        def _():
            part_copy(1).start()
            part_copy(2).start()
            r_copy().start()

        @pl.when(bends)
        def _():
            bend_copy(0).start()
            bend_copy(1).start()

    def map_send():
        @pl.when(bends)
        def _():
            r_copy().start()

    def part_copy(k):
        js = pl.ds(0, 2) if k == 0 else pl.ds(1 + k, 1)
        return remote(LS.at[1, js], LR.at[1, js], lat_s.at[1 + k], lat_r.at[1 + k], {"lat": lax.rem(lat + 1, lats)})

    def bend_copy(k):
        peer = {"lat": lax.rem(lat + lats - (xs - 1 if k else 1), lats)}
        return remote(LS.at[1, pl.ds(2 + k, 1)], RL, lat_s.at[2 + k], rl_r, peer)

    def relay_copy(k):
        peer = {"lat": lax.rem(lat + (xs if k else 2), lats)}
        return remote(RL, LR.at[1, pl.ds(2 + k, 1)], rl_s, lat_r.at[2 + k], peer)

    def pass_on(k):
        @pl.when(starts if k else relays)
        def _():
            bend_copy(k).wait_recv()
            relay_copy(k).start()

    def lag(c):
        for j in range(rows):
            x = solved(c, j)
            if c == 0:
                hi, lo = split(value_trace(x))
                LAT[0, 1, j] = hi
                LAT[1, 1, j] = lo
            put_source(c, j, x)

    def finish(c):
        for j in range(rows):
            out[c, 0, j] = solved(c, j).astype(BF16)

    def lat_arrival(it):
        @pl.when(lat > 0)
        def _():
            if it == 0:
                lat_copy(it).wait_recv()
            else:
                for k in range(3):
                    part_copy(k).wait_recv()
                r_copy().wait_recv()
                x_copy().wait_recv()
                xh, xl = split(XL[...])
            for j in range(rows):
                trace = LR[it, j]
                if it == 1:
                    rh, rl = split(RR[j // 2][:, (j % 2) * face : (j % 2 + 1) * face])
                    trace = trace + (dot(rh, xh) + (dot(rl, xh) + dot(rh, xl)))
                hi, lo = split(trace)
                LAT[0, 0, j] = hi
                LAT[1, 0, j] = lo

        @pl.when(lat == 0)
        def _():
            for j in range(rows):
                LAT[0, 0, j] = zero_trace
                LAT[1, 0, j] = zero_trace

    def prefix_maps():
        for d in (1, 3, 2):
            tc_arrival(d).wait_recv()
        width = (YS + 1) * face
        row_id = lax.broadcasted_iota(jnp.int32, (face, width), 0)
        lane_id = lax.broadcasted_iota(jnp.int32, (face, width), 1)

        def unit(block):
            return jnp.where(lane_id - face * block == row_id, 1.0, 0.0).astype(F32)

        for c in range(cols):
            x = unit(YS)
            mine = jnp.where(y == 0, x, jnp.zeros_like(x))
            for t in range(YS):
                if t == 0:
                    x = cat_lanes(TC[0, c], width) + unit(0)
                else:
                    th, tl = split(TC[t, c])
                    x = dot3(th, tl, x) + unit(t)
                if t + 1 < YS:
                    mine = jnp.where(y == t + 1, x, mine)
            both = dot3(THL[0, c, 0], THL[0, c, 1], mine)
            vh, vl = split(cat0(mine, both, x))
            VV[c, 0] = vh
            VV[c, 1] = vl
            v = slice(YS * face, (YS + 1) * face)
            VO[c, 0] = jnp.where(is0, vh[0:face, v], vh[face : 2 * face, v])
            VO[c, 1] = jnp.where(is0, vl[0:face, v], vl[face : 2 * face, v])

    first_source(1)

    t_copy.wait_recv()
    for c in range(cols):
        own, got = TT[c], TP[c]
        t0h, t0l = split(jnp.where(is0, own, got))
        t1h, t1l = split(jnp.where(is0, got, own))
        THL[0, c, 0], THL[0, c, 1], THL[1, c, 0], THL[1, c, 1] = t0h, t0l, t1h, t1l
        TC[y, c] = dot3(t1h, t1l, jnp.where(is0, own, got))

    def tc_copy(d):
        return remote(TC.at[y], TC.at[y], tc_s.at[d - 1], tc_r.at[y], ypeer(d))

    def tc_arrival(d):
        source = lax.rem(y + d, YS)
        return remote(TC.at[source], TC.at[source], tc_s.at[d - 1], tc_r.at[source], ypeer(d))

    for d in (2, 1, 3):
        tc_copy(d).start()

    chain(0, 1)
    first_source(0)
    compose(0, 1)
    loads["ar1"].wait()
    traces_ahead()
    maps_rest(1)

    early, late = range(0, 2), range(2, rows)
    lat_arrival(0)
    chain(0, 0)
    rest(1, early)
    compose(0, 0)
    prefix_maps()
    gather(0, 1)
    map_send()
    rest(1, late)

    @pl.when(zhi == 0)
    def _():
        enter(0, 1)

    pass_on(0)
    loads["ar0"].wait()
    maps_rest(0)
    rest(0, early)
    gather(0, 0)
    pass_on(1)
    rest(0, late)

    @pl.when(zhi == 1)
    def _():
        enter(0, 1)

    inflows(0, 1)
    lag(1)
    enter(0, 0)
    inflows(0, 0)
    lag(0)
    lat_arrival(1)

    chain(1, 0, 1)
    compose(1, 0)
    compose(1, 1)
    rest(0, range(rows))
    rest(1, range(rows))

    def sent(it):
        for c in range(cols):
            s1_copy(it, c).wait_send()
            s4_copy(it, c).wait_send()
            for d in range(1, YS):
                s2_copy(it, c, d).wait_send()

        @pl.when(zhi == 0)
        def _():
            for c in range(cols):
                for k in range(2):
                    z_copy(it, c, k).wait_send()

        @pl.when(lat < lats - 1)
        def _():
            if it == 0:
                lat_copy(it).wait_send()
            else:
                for k in range(3):
                    part_copy(k).wait_send()

        if it == 1:

            for k in range(2):

                @pl.when(starts if k else relays)
                def _():
                    relay_copy(k).wait_send()

    t_copy.wait_send()
    for d in range(1, YS):
        tc_copy(d).wait_send()

    @pl.when(lat < lats - 1)
    def _():
        x_copy().wait_send()
        r_copy().wait_send()

    sent(0)
    gather(1, 0)
    gather(1, 1)
    enter(1, 0)
    inflows(1, 0)
    finish(0)
    enter(1, 1)
    inflows(1, 1)
    finish(1)
    sent(1)


def cat_lanes(t, width):
    face = t.shape[0]
    return jnp.concatenate([jnp.zeros((face, width - face), F32), t], axis=1)


def per_device(inverse, upwind, lateral, inlet_trace, previous, uptake_rate, affinity, flow_order):
    operands = (flow_order, inverse, upwind, lateral, inlet_trace, previous, uptake_rate, affinity)
    hbm = pl.BlockSpec(memory_space=pltpu.HBM)
    vmem = pl.BlockSpec(memory_space=pltpu.VMEM)
    dma = pltpu.SemaphoreType.DMA
    scratch = [
        pltpu.SMEM((2, 1, 4), jnp.int32),
        pltpu.VMEM((2, 64, 256), F32),
        pltpu.VMEM((256,), F32),
        pltpu.VMEM((256,), F32),
        pltpu.VMEM((2, 4, 512, 512), BF16),
        pltpu.VMEM((2, 4, 256, 512), BF16),
        pltpu.VMEM((2, 4, 512, 256), BF16),
        pltpu.VMEM((2, 4, 512, 256), BF16),
        pltpu.VMEM((2, 4, 512, 256), BF16),
        pltpu.VMEM((2, 4, 512, 256), F32),
        pltpu.VMEM((2, 2, 4, 512, 256), BF16),
        pltpu.VMEM((2, 4, 64, 256), F32),
        pltpu.VMEM((2, 4, 64, 256), F32),
        pltpu.VMEM((2, 2, 4, 64, 256), BF16),
        pltpu.VMEM((2, 3, 64, 256), F32),
        pltpu.VMEM((2, 2, 4, 64, 64), BF16),
        pltpu.VMEM((2, 2, 4, 64, 256), BF16),
        pltpu.VMEM((2, 64, 64), F32),
        pltpu.VMEM((2, 64, 64), F32),
        pltpu.VMEM((4, 2, 64, 64), F32),
        pltpu.VMEM((2, 2, 2, 64, 64), BF16),
        pltpu.VMEM((2, 2, 192, 320), BF16),
        pltpu.VMEM((2, 2, 2, 64, 128), F32),
        pltpu.VMEM((2, 2, 64, 128), F32),
        pltpu.VMEM((2, 2, 5, 64, 128), F32),
        pltpu.VMEM((2, 2, 64, 128), F32),
        pltpu.VMEM((2, 2, 2, 64, 128), F32),
        pltpu.VMEM((2, 2, 64, 128), F32),
        pltpu.VMEM((2, 2, 2, 64, 128), F32),
        pltpu.VMEM((2, 2, 64, 64), BF16),
        pltpu.VMEM((2, 2, 64, 256), F32),
        pltpu.VMEM((64, 256), F32),
        pltpu.VMEM((2, 64, 128), F32),
        pltpu.VMEM((2, 64, 128), F32),
        pltpu.VMEM((1, 64, 256), F32),
        dma((18,)),
        dma((4,)), dma((4,)),
        dma, dma,
        dma((3,)), dma((4,)),
        dma((2, 2)), dma((2, 2)),
        dma((2, 2, 3)), dma((2, 2, 4)),
        dma((2, 2, 2)), dma((2, 2, 2)),
        dma((2, 2)), dma((2, 2)),
        dma, dma, dma, dma,
        dma, dma,
        pltpu.SemaphoreType.REGULAR,
    ]
    return pl.pallas_call(
        kernel,
        out_shape=jax.ShapeDtypeStruct(previous.shape, BF16),
        in_specs=[hbm] * 8,
        out_specs=vmem,
        scratch_shapes=scratch,
        compiler_params=pltpu.CompilerParams(
            collective_id=0, has_side_effects=True, vmem_limit_bytes=40 * 1024 * 1024
        ),
    )(*(pltpu.with_memory_space_constraint(a, pltpu.HBM) for a in operands))


def solution(mesh):
    placed = (
        P("lat", "stream", None, None, None),
        P("lat", "stream", None, None, None),
        P("lat", "stream", None, None, None),
        P("lat", None, None),
        P("lat", "stream", None, None, None),
        P(),
        P(),
        P("lat", "stream", None),
    )
    return jax.shard_map(
        per_device,
        mesh=mesh,
        in_specs=placed,
        out_specs=P("lat", "stream", None, None, None),
        check_vma=False,
    )
```
